32 devices in a mesh: dp: 4 (over y, core), row: 4 (over z), view: 2 (over x).
Axes of the slice: x: 2, y: 2, z: 4, core: 2. Of those that a mesh axis runs over, the one named last changes fastest.
Arguments:
- frames_in: float32 [2, 4, 64, 16, 480], P('view', 'dp', None, 'row'), may hold values from -13 to 13
- cotangent: float32 [2, 4, 64, 16, 480], P('view', 'dp', None, 'row'), may hold values from -36 to 36
- expand_in: float32 [128, 64], replicated, may hold values from -0.75 to 0.75
- conv_kernel: float32 [128, 3, 3], replicated, may hold values from -2 to 2
- pool_proj: float32 [64, 64], replicated, may hold values from -1.5 to 1.5
- pool_bias: float32 [64], replicated, may hold values from 0.5 to 1.5
- squeeze_out: float32 [64, 64], replicated, may hold values from -0.75 to 0.75
- branch_scale: float32 [64], replicated, may hold values from 0.3 to 1
- ffn_expand: float32 [128, 64], replicated, may hold values from -0.75 to 0.75
- ffn_shrink: float32 [64, 64], replicated, may hold values from -0.75 to 0.75
- ffn_scale: float32 [64], replicated, may hold values from 0.3 to 1
- query_proj: float32 [2, 64, 64], P('view'), may hold values from -1.5 to 1.5
- value_proj: float32 [2, 64, 64], P('view'), may hold values from -0.75 to 0.75
- cross_scale: float32 [2, 64], P('view'), may hold values from 0.3 to 1
Outputs:
- block_out: float32 [2, 4, 64, 16, 480], P('view', 'dp', None, 'row')
- grad_in: float32 [2, 4, 64, 16, 480], P('view', 'dp', None, 'row')
- grad_expand: float32 [128, 64], replicated
- grad_kernel: float32 [128, 3, 3], replicated
- grad_pool: float32 [64, 64], replicated
- grad_bias: float32 [64], replicated
- grad_squeeze: float32 [64, 64], replicated
- grad_branch: float32 [64], replicated
- grad_ffn_up: float32 [128, 64], replicated
- grad_ffn_down: float32 [64, 64], replicated
- grad_ffn_scale: float32 [64], replicated
- grad_query: float32 [2, 64, 64], P('view')
- grad_value: float32 [2, 64, 64], P('view')
- grad_cross: float32 [2, 64], P('view')
The draws below stay inside these ranges and needn't reach their ends.
All inputs are finite; a program needn't handle non-finite values.
Results may differ from the reference program's by a relative error of at most 0.0003.
Values sent between devices are 32-bit elements; how exact they have to be, the bound alone decides.
No kernel may reach another device: no remote copies, remote signals or barrier semaphores. Data moves between devices by JAX's collectives and lax.ppermute only.
A program may use at most 64 MiB of HBM per device.

```python
import jax
import jax.numpy as jnp
from jax import lax

CH = 64
COLS = 480
FRAMES = 4
HEIGHT = 16


def draw_frames_in(key, part):
    noise_key, pattern_key = jax.random.split(jax.random.fold_in(key, 11))
    shape = (2, FRAMES, CH, HEIGHT, COLS)
    pattern = jnp.clip(jax.random.normal(pattern_key, (CH,), jnp.float32), -3.0, 3.0)
    ramp = jnp.arange(HEIGHT, dtype=jnp.float32) * (2.0 / max(HEIGHT - 1, 1))
    noise = jnp.clip(jax.random.normal(noise_key, shape, jnp.float32), -5.0, 5.0)
    return noise + pattern[None, None, :, None, None] * ramp[None, None, None, :, None]


def draw_cotangent(key, part):
    noise_key = jax.random.fold_in(key, 23)
    shape = (2, FRAMES, CH, HEIGHT, COLS)
    frame_rise = 1.0 + jnp.arange(FRAMES, dtype=jnp.float32) * (2.0 / max(FRAMES - 1, 1))
    row_rise = 1.0 + jnp.arange(HEIGHT, dtype=jnp.float32) * (2.0 / max(HEIGHT - 1, 1))
    noise = jnp.clip(jax.random.normal(noise_key, shape, jnp.float32), -4.0, 4.0)
    return noise * frame_rise[None, :, None, None, None] * row_rise[None, None, None, :, None]


def block_scale(stream_key, extent, shards, smallest, largest):
    def one(position, shards_of):
        steps = jax.random.uniform(jax.random.fold_in(jax.random.fold_in(stream_key, 6), position), (shards_of,), jnp.float32, smallest / len(shards), largest / len(shards))
        return jnp.repeat(jnp.exp(steps), extent[position] // shards_of).reshape((-1,) + (1,) * (len(extent) - position - 1))

    gain = one(*shards[0])
    for cut in shards[1:]:
        gain = gain * one(*cut)
    return gain


def gaussian(key, extent, scale, bound, pieces=(), kind=jnp.bfloat16):
    factor_of = block_scale(key, extent, pieces, -0.22, 0.18) if pieces else 1.0
    array = jax.random.normal(key, extent, jnp.float32) * scale * factor_of
    return jnp.minimum(jnp.maximum(array, -bound), bound).astype(kind)


def setup_inputs(seed: int = 0) -> dict:
    key_of = jax.random.split(jax.random.key(seed), 15)
    return {
        "frames_in": draw_frames_in(jax.random.fold_in(key_of[14], 71), 0),
        "cotangent": draw_cotangent(jax.random.fold_in(key_of[14], 71), 0),
        "expand_in": gaussian(key_of[2], (2 * CH, CH), CH ** -0.5, 0.75, (), jnp.float32),
        "conv_kernel": gaussian(key_of[3], (2 * CH, 3, 3), 9 ** -0.5, 2.0, (), jnp.float32),
        "pool_proj": gaussian(key_of[4], (CH, CH), (CH // 4) ** -0.5, 1.5, (), jnp.float32),
        "pool_bias": jnp.clip(1.0 + 0.1 * jax.random.normal(key_of[5], (CH,), jnp.float32), 0.5, 1.5),
        "squeeze_out": gaussian(key_of[6], (CH, CH), CH ** -0.5, 0.75, (), jnp.float32),
        "branch_scale": jnp.clip(jax.random.uniform(key_of[7], (CH,), jnp.float32, 0.3, 1.0), 0.3, 1.0),
        "ffn_expand": gaussian(key_of[8], (2 * CH, CH), CH ** -0.5, 0.75, (), jnp.float32),
        "ffn_shrink": gaussian(key_of[9], (CH, CH), CH ** -0.5, 0.75, (), jnp.float32),
        "ffn_scale": jnp.clip(jax.random.uniform(key_of[10], (CH,), jnp.float32, 0.3, 1.0), 0.3, 1.0),
        "query_proj": gaussian(key_of[11], (2, CH, CH), (CH // 4) ** -0.5, 1.5, ((0, 2),), jnp.float32),
        "value_proj": gaussian(key_of[12], (2, CH, CH), CH ** -0.5, 0.75, ((0, 2),), jnp.float32),
        "cross_scale": jnp.clip(0.3 + 0.7 * jax.random.uniform(key_of[13], (2, CH), jnp.float32) ** block_scale(key_of[13], (2, CH), ((0, 2),), -0.2, 0.2), 0.3, 1.0),
    }


epsilon = 1e-06
highest = lax.Precision.HIGHEST

def channel_norm(fields):
    center = fields - lax.optimization_barrier(jnp.mean(fields, axis=-3, keepdims=True))
    spread = lax.optimization_barrier(jnp.mean(center * center, axis=-3, keepdims=True))
    return center / jnp.sqrt(spread + epsilon)

def mixing(weight, fields):
    return jnp.einsum('oc,...chw->...ohw', weight, fields, precision=highest)

def depthwise(padded, kernel, height, breadth):
    summed = kernel[:, 0, 0][:, None, None] * padded[..., 0:height, 0:breadth]
    for offset in range(1, 9):
        row_off = offset // 3
        col_off = offset % 3
        summed = summed + kernel[:, row_off, col_off][:, None, None] * padded[..., row_off:row_off + height, col_off:col_off + breadth]
    return summed

def simple_gate(doubled):
    halves = doubled.shape[-3] // 2
    return doubled[..., :halves, :, :] * doubled[..., halves:, :, :]

def attend(hidden, queries, query_other, value_other, scales):
    scores = jnp.einsum('...chi,...chj->...hij', queries, query_other, precision=highest) * queries.shape[-3] ** (-0.5)
    weights = jnp.exp(scores)
    weights = weights / lax.optimization_barrier(jnp.sum(weights, axis=-1, keepdims=True))
    carried = jnp.einsum('...hij,...chj->...chi', weights, value_other, precision=highest)
    return hidden + scales[:, None, None] * carried

def block_tail(frames, gating, pooled, pool_proj, pool_bias, squeeze_out, branch_scale, ffn_expand, ffn_shrink, ffn_scale):
    attention = jnp.einsum('oc,...c->...o', pool_proj, pooled, precision=highest) + pool_bias
    scaled = gating * attention[..., :, None, None]
    residual_one = frames + branch_scale[:, None, None] * mixing(squeeze_out, scaled)
    expanded = mixing(ffn_expand, channel_norm(residual_one))
    return residual_one + ffn_scale[:, None, None] * mixing(ffn_shrink, simple_gate(expanded))

def one_view(frames, params):
    doubled = mixing(params[0], channel_norm(frames))
    padded = jnp.pad(doubled, ((0, 0), (1, 1), (1, 1)))
    gating = simple_gate(depthwise(padded, params[1], HEIGHT, COLS))
    pooled = lax.optimization_barrier(jnp.sum(gating, axis=(1, 2))) / (HEIGHT * COLS)
    return block_tail(frames, gating, pooled, params[2], params[3], params[4], params[5], params[6], params[7], params[8])

def frame_pair(paired, params):
    query_proj, value_proj, cross_scale = (params[9], params[10], params[11])
    hidden = [one_view(paired[view_idx], params) for view_idx in range(2)]
    queries = [mixing(query_proj[view_idx], channel_norm(hidden[view_idx])) for view_idx in range(2)]
    values = [mixing(value_proj[view_idx], hidden[view_idx]) for view_idx in range(2)]
    results = [attend(hidden[view_idx], queries[view_idx], queries[1 - view_idx], values[1 - view_idx], cross_scale[view_idx]) for view_idx in range(2)]
    return jnp.stack(results)

def reference(frames_in, cotangent, expand_in, conv_kernel, pool_proj, pool_bias, squeeze_out, branch_scale, ffn_expand, ffn_shrink, ffn_scale, query_proj, value_proj, cross_scale):
    params = (expand_in, conv_kernel, pool_proj, pool_bias, squeeze_out, branch_scale, ffn_expand, ffn_shrink, ffn_scale, query_proj, value_proj, cross_scale)

    def step_frame(carry, paired):
        inputs_now, upstream = paired
        output, backward = jax.vjp(frame_pair, inputs_now, params)
        grad_frame, grad_params = backward(upstream)
        return (jax.tree.map(jnp.add, carry, grad_params), (output, grad_frame))
    zeroes = jax.tree.map(jnp.zeros_like, params)
    inputs_all = jnp.moveaxis(frames_in, 1, 0)
    upstream_all = jnp.moveaxis(cotangent, 1, 0)
    totals, (outputs, grads_all) = lax.scan(step_frame, zeroes, (inputs_all, upstream_all))
    factor = (2 * FRAMES * HEIGHT * COLS) ** (-0.5)
    scaled = [grad_item * factor for grad_item in totals]
    return (jnp.moveaxis(outputs, 0, 1), jnp.moveaxis(grads_all, 0, 1), scaled[0], scaled[1], scaled[2], scaled[3], scaled[4], scaled[5], scaled[6], scaled[7], scaled[8], scaled[9], scaled[10], scaled[11])
```

```python
import functools

import jax
import jax.numpy as jnp
from jax import lax
from jax.experimental import pallas as pl
from jax.experimental.pallas import tpu as pltpu
from jax.sharding import PartitionSpec as P

epsilon = 1e-06
F32 = jnp.float32
BF16 = jnp.bfloat16
MIB = 1 << 20


def split(x):
    high = x.astype(BF16)
    return high, (x - high.astype(F32)).astype(BF16)


def stack_rows(*parts):
    return jnp.concatenate(parts, axis=0)


def left_rows(w):
    h, l = split(w)
    return stack_rows(h, h, l)


def right_rows(x):
    h, l = split(x)
    return stack_rows(h, l, h)


def left_lanes(w):
    h, l = split(w)
    return jnp.concatenate([h, h, l], axis=1)


def dot_nn(a, b):
    return lax.dot_general(a, b, (((1,), (0,)), ((), ())), preferred_element_type=F32)


def dot_tn(a, b):
    return lax.dot_general(a, b, (((0,), (0,)), ((), ())), preferred_element_type=F32)


def dot_nt(a, b):
    return lax.dot_general(a, b, (((1,), (1,)), ((), ())), preferred_element_type=F32)


def outer_pixels(a, b):
    return dot_nt(stack_rows(*split(a)), stack_rows(*split(b)))


def fold(acc):
    m, n = acc.shape[0] // 2, acc.shape[1] // 2
    return acc[:m, :n] + acc[:m, n:] + acc[m:, :n]


def channel_mean(x):
    return jnp.sum(x, axis=0, keepdims=True) * (1.0 / x.shape[0])


def normed_of(x):
    center = x - channel_mean(x)
    scale = 1.0 / jnp.sqrt(channel_mean(center * center) + epsilon)
    return center * scale, scale


def norm_back(grad, normed, scale):
    return scale * (grad - channel_mean(grad) - normed * channel_mean(grad * normed))


def eye(n):
    rows = lax.broadcasted_iota(jnp.int32, (n, n), 0)
    return (rows == lax.broadcasted_iota(jnp.int32, (n, n), 1)).astype(F32)


def to_column(row):
    return jnp.sum(eye(row.shape[1]) * row, axis=1, keepdims=True)


def to_row(column):
    return jnp.sum(eye(column.shape[0]) * column, axis=0, keepdims=True)


def lane_mask(shape, width):
    return lax.broadcasted_iota(jnp.int32, shape, len(shape) - 1) < width


def relayout(x_ref, o_ref):
    rows, width = o_ref.shape[0], x_ref.shape[2]
    padded = o_ref.shape[2]
    for h in range(rows):
        o_ref[h, :, 0:width] = x_ref[:, h, :]
        if padded > width:
            o_ref[h, :, width:padded] = jnp.zeros((o_ref.shape[1], padded - width), F32)


def start_kernel(x_ref, q_ref, v_ref, s_ref, band_ref, first_ref, last_ref, pack_ref):
    ch = q_ref.shape[0]
    relayout(x_ref, band_ref)
    first_ref[...] = band_ref[0]
    last_ref[...] = band_ref[band_ref.shape[0] - 1]
    pack_ref[0:ch, 0:ch] = q_ref[...]
    pack_ref[0:ch, ch : 2 * ch] = v_ref[...]
    pack_ref[ch : ch + 8, 0:ch] = jnp.broadcast_to(s_ref[...], (8, ch))


def kernel_columns(k_ref, kt_ref):
    tall = k_ref.shape[2]
    rows = lax.broadcasted_iota(jnp.int32, (tall, tall), 0)
    mat = jnp.zeros((tall, tall), F32)
    for i in range(3):
        for j in range(3):
            mat = jnp.where(rows == 3 * i + j, k_ref[i, j : j + 1, :], mat)
    kt_ref[...] = mat.T


def shifted(x):
    n = x.shape[1]
    return pltpu.roll(x, 1, 1), x, pltpu.roll(x, n - 1, 1)


def conv_own_kernel(
    view_ref, band_ref, exp_ref, k_ref, cot_ref, doubled_ref, conv_ref, send_ref, keep_ref, kt_ref, cband_ref
):
    rows, ch, padded = band_ref.shape
    half = rows // 2
    wide = doubled_ref.shape[1]
    kernel_columns(k_ref, kt_ref)
    weight = left_rows(exp_ref[...])
    for h in range(rows):
        doubled_ref[h] = dot_tn(weight, right_rows(normed_of(band_ref[h])[0]))

    def group(g, carry):
        at = pl.ds(pl.multiple_of(g * 8, 8), 8)
        taps = kt_ref[at, :]
        moved = [shifted(doubled_ref[h, at, :]) for h in range(rows)]
        for h in range(rows):
            total = None
            for i in range(3):
                src = h + i - 1
                if 0 <= src < rows:
                    for j in range(3):
                        term = taps[:, 3 * i + j : 3 * i + j + 1] * moved[src][j]
                        total = term if total is None else total + term
            conv_ref[h, at, :] = total
        return carry

    lax.fori_loop(0, wide // 8, group, 0)
    relayout(cot_ref, cband_ref)
    view = view_ref[0]
    for k in range(half):
        keep_ref[k] = cband_ref[half * view + k]
        send_ref[k] = cband_ref[half * (1 - view) + k]


def conv_edge_kernel(
    width, part_ref, doubled_ref, up_ref, down_ref, exp_ref, k_ref, conv_ref, edge_ref, gating_ref, pool_ref, kt_ref
):
    rows, wide, padded = part_ref.shape
    ch = wide // 2
    kernel_columns(k_ref, kt_ref)
    weight = left_rows(exp_ref[...])
    edge_ref[0] = dot_tn(weight, right_rows(normed_of(up_ref[...])[0]))
    edge_ref[1] = dot_tn(weight, right_rows(normed_of(down_ref[...])[0]))
    keep = lane_mask((8, padded), width)

    def group(g, carry):
        lower = pl.multiple_of(g * 8, 8)
        halves = []
        for offset in (0, ch):
            at = pl.ds(pl.multiple_of(lower + offset, 8), 8)
            taps = kt_ref[at, :]
            above, below = shifted(edge_ref[0, at, :]), shifted(edge_ref[1, at, :])
            out = []
            for h in range(rows):
                total = part_ref[h, at, :]
                for j in range(3):
                    if h == 0:
                        total = total + taps[:, j : j + 1] * above[j]
                    if h == rows - 1:
                        total = total + taps[:, 6 + j : 7 + j] * below[j]
                total = jnp.where(keep, total, 0.0)
                conv_ref[h, at, :] = total
                out.append(total)
            halves.append(out)
        pooled = jnp.zeros((8, padded), F32)
        at = pl.ds(lower, 8)
        for h in range(rows):
            gate = halves[0][h] * halves[1][h]
            gating_ref[h, at, :] = gate
            pooled = pooled + gate
        kt_ref[at, :] = jnp.broadcast_to(jnp.sum(pooled, axis=1, keepdims=True), (8, kt_ref.shape[1]))
        return carry

    lax.fori_loop(0, ch // 8, group, 0)
    sums = to_row(kt_ref[0:ch, 0:1])
    pool_ref[...] = jnp.zeros(pool_ref.shape, F32)
    pool_ref[:, 0:ch] = jnp.broadcast_to(sums, (8, ch))


def attention_of(pool_ref, proj_ref, bias_ref, area):
    ch = proj_ref.shape[0]
    pooled = pool_ref[:, 0:ch] * (1.0 / area)
    ph, plow = split(pooled)
    wh, wl = split(proj_ref[...])
    product = dot_nt(ph, wh) + dot_nt(ph, wl) + dot_nt(plow, wh)
    return pooled[0:1], product[0:1] + bias_ref[...]


def tail_kernel(
    area,
    base_ref,
    band_ref,
    gating_ref,
    pool_ref,
    proj_ref,
    bias_ref,
    squeeze_ref,
    branch_ref,
    up_ref,
    down_ref,
    scale_ref,
    hidden_ref,
    one_ref,
    expanded_ref,
):
    half, ch, _ = hidden_ref.shape
    _, attention = attention_of(pool_ref, proj_ref, bias_ref, area)
    squeeze = left_lanes(to_column(branch_ref[...]) * squeeze_ref[...] * attention)
    up = left_rows(up_ref[...])
    down = left_lanes(to_column(scale_ref[...]) * down_ref[...])
    base = base_ref[0]
    for k in range(half):
        one = band_ref[base + k] + dot_nn(squeeze, right_rows(gating_ref[base + k]))
        one_ref[k] = one
        expanded = dot_tn(up, right_rows(normed_of(one)[0]))
        expanded_ref[k] = expanded
        hidden_ref[k] = one + dot_nn(down, right_rows(expanded[:ch] * expanded[ch:]))


def attend_kernel(
    width,
    hid0_ref,
    hid1_ref,
    cot0_ref,
    cot1_ref,
    pack0_ref,
    pack1_ref,
    out0_ref,
    out1_ref,
    dh0_ref,
    dh1_ref,
    grad0_ref,
    grad1_ref,
    e_ref,
    eh_ref,
    el_ref,
):
    half, ch, padded = hid0_ref.shape
    block = 128
    inv = ch ** (-0.5)
    mask = lane_mask((1, padded), width)
    hids, cots = (hid0_ref, hid1_ref), (cot0_ref, cot1_ref)
    wq = [ref[0:ch, 0:ch] for ref in (pack0_ref, pack1_ref)]
    wv = [ref[0:ch, ch : 2 * ch] for ref in (pack0_ref, pack1_ref)]
    scale = [to_column(ref[ch : ch + 1, 0:ch]) for ref in (pack0_ref, pack1_ref)]
    lq, lv = [left_lanes(w) for w in wq], [left_lanes(w) for w in wv]
    lqt, lvt = [left_rows(w) for w in wq], [left_rows(w) for w in wv]
    acc_q, acc_v, acc_s = [None, None], [None, None], [None, None]

    def add(acc, s, value):
        acc[s] = value if acc[s] is None else acc[s] + value

    for k in range(half):
        h = [ref[k] for ref in hids]
        u = [ref[k] for ref in cots]
        norms = [normed_of(x) for x in h]
        q = [dot_nn(lq[s], right_rows(norms[s][0])) for s in range(2)]
        v = [dot_nn(lv[s], right_rows(h[s])) for s in range(2)]
        qh, ql = zip(*[split(q[0] * inv), split(q[1])])
        vh, vl = zip(*[split(x) for x in v])
        left = stack_rows(qh[0], qh[0], ql[0])
        right = stack_rows(qh[1], ql[1], qh[1])
        col_sum = jnp.zeros((1, padded), F32)
        for b in range(0, padded, block):
            scores = dot_tn(left[:, b : b + block], right)
            weights = jnp.where(mask, jnp.exp(scores), 0.0)
            if b + block > width:
                rows_at = lax.broadcasted_iota(jnp.int32, (block, 1), 0) + b
                weights = jnp.where(rows_at < width, weights, 0.0)
            eh, el = split(weights)
            e_ref[b : b + block, :] = weights
            eh_ref[b : b + block, :] = eh
            el_ref[b : b + block, :] = el
            col_sum = col_sum + jnp.sum(weights, axis=0, keepdims=True)
        b_inv = jnp.where(mask, 1.0 / jnp.where(mask, col_sum, 1.0), 0.0)
        g = [scale[s] * u[s] for s in range(2)]
        bg = g[1] * b_inv
        bgh, bgl = split(bg)
        ones = jnp.ones((16, padded), BF16)
        first = dot_nt(stack_rows(vh[1], vl[1], bgh, bgl, ones), eh_ref[...])
        second = dot_nt(stack_rows(vh[1], bgh, ones), el_ref[...])
        row_sum = first[4 * ch : 4 * ch + 1] + second[2 * ch : 2 * ch + 1]
        a_inv = jnp.where(mask, 1.0 / jnp.where(mask, row_sum, 1.0), 0.0)
        carried0 = (first[0:ch] + first[ch : 2 * ch] + second[0:ch]) * a_inv
        dv0 = first[2 * ch : 3 * ch] + first[3 * ch : 4 * ch] + second[ch : 2 * ch]
        ag = g[0] * a_inv
        agh, agl = split(ag)
        first = dot_nn(stack_rows(vh[0], vl[0], agh, agl), eh_ref[...])
        second = dot_nn(stack_rows(vh[0], agh), el_ref[...])
        carried1 = (first[0:ch] + first[ch : 2 * ch] + second[0:ch]) * b_inv
        dv1 = first[2 * ch : 3 * ch] + first[3 * ch : 4 * ch] + second[ch : 2 * ch]
        out0_ref[k] = h[0] + scale[0] * carried0
        out1_ref[k] = h[1] + scale[1] * carried1
        d0 = jnp.sum(ag * carried0, axis=0, keepdims=True)
        d1 = jnp.sum(bg * carried1, axis=0, keepdims=True)
        d0h, d0l = split(d0)
        row_at = lax.broadcasted_iota(jnp.int32, (16, padded), 0)
        extra = jnp.where(row_at == 0, d0h.astype(F32), jnp.where(row_at == 1, d0l.astype(F32), 0.0)).astype(BF16)
        left = stack_rows(agh, vh[0], agh, vh[0], agl, vl[0], extra)
        right = stack_rows(vh[1], bgh, vl[1], bgl, vh[1], bgh, -ones)
        for b in range(0, padded, block):
            inner = dot_tn(left[:, b : b + block], right) - d1
            dsh, dsl = split(e_ref[b : b + block, :] * inner)
            eh_ref[b : b + block, :] = dsh
            el_ref[b : b + block, :] = dsl
        first = dot_nt(stack_rows(qh[1], ql[1]), eh_ref[...])
        dq0 = (first[0:ch] + first[ch : 2 * ch] + dot_nt(qh[1], el_ref[...])) * inv
        first = dot_nn(stack_rows(qh[0], ql[0]), eh_ref[...])
        dq1 = first[0:ch] + first[ch : 2 * ch] + dot_nn(qh[0], el_ref[...])
        dq, dv, carried = (dq0, dq1), (dv0, dv1), (carried0, carried1)
        for s, ref in enumerate((dh0_ref, dh1_ref)):
            normed, spread = norms[s]
            dn = dot_tn(lqt[s], right_rows(dq[s]))
            ref[k] = u[s] + norm_back(dn, normed, spread) + dot_tn(lvt[s], right_rows(dv[s]))
            add(acc_q, s, outer_pixels(dq[s], normed))
            add(acc_v, s, outer_pixels(dv[s], h[s]))
            add(acc_s, s, u[s] * carried[s])
    for s, ref in enumerate((grad0_ref, grad1_ref)):
        ref[0:ch, 0:ch] = fold(acc_q[s])
        ref[0:ch, ch : 2 * ch] = fold(acc_v[s])
        row = to_row(jnp.sum(acc_s[s], axis=1, keepdims=True))
        ref[ch : ch + 8, 0:ch] = jnp.broadcast_to(row, (8, ch))
        ref[ch : ch + 8, ch : 2 * ch] = jnp.zeros((8, ch), F32)


def tail_back_kernel(
    area,
    final,
    base_ref,
    dh_ref,
    one_ref,
    expanded_ref,
    gating_ref,
    pool_ref,
    proj_ref,
    bias_ref,
    squeeze_ref,
    branch_ref,
    up_ref,
    down_ref,
    scale_ref,
    *refs,
):
    half, ch, _ = dh_ref.shape
    base = base_ref[0]
    pooled, attention = attention_of(pool_ref, proj_ref, bias_ref, area)
    branch, scale = to_column(branch_ref[...]), to_column(scale_ref[...])
    mixed = branch * squeeze_ref[...]
    squeeze = left_rows(mixed * attention)
    up = left_lanes(up_ref[...])
    down = left_rows(scale * down_ref[...])
    if final:
        acc_in, dgate_in, done_in, (dgate_ref, done_ref, pg_ref, grad_ref) = refs[0], refs[1], refs[2], refs[3:]
    else:
        dgate_ref, done_ref, acc_ref = refs
    acc1 = acc2 = acc3 = None
    for k in range(half):
        dh, one, expanded = dh_ref[k], one_ref[k], expanded_ref[k]
        lower, upper = expanded[:ch], expanded[ch:]
        normed, spread = normed_of(one)
        term1 = outer_pixels(dh, lower * upper)
        dprod = dot_tn(down, right_rows(dh))
        dexp = stack_rows(dprod * upper, dprod * lower)
        term2 = outer_pixels(normed, dexp)
        dn = dot_nn(up, right_rows(dexp))
        done = dh + norm_back(dn, normed, spread)
        done_ref[k] = done
        term3 = outer_pixels(done, gating_ref[base + k])
        dgate_ref[k] = dot_tn(squeeze, right_rows(done))
        acc1 = term1 if acc1 is None else acc1 + term1
        acc2 = term2 if acc2 is None else acc2 + term2
        acc3 = term3 if acc3 is None else acc3 + term3
    if not final:
        acc_ref[:, 0 : 2 * ch] = acc1
        acc_ref[:, 2 * ch : 6 * ch] = acc2
        acc_ref[:, 6 * ch : 8 * ch] = acc3
        return
    m1 = fold(acc1 + acc_in[:, 0 : 2 * ch])
    m2 = fold(acc2 + acc_in[:, 2 * ch : 6 * ch])
    m3 = fold(acc3 + acc_in[:, 6 * ch : 8 * ch])
    datt = jnp.sum(mixed * m3, axis=0, keepdims=True)
    dcol = to_column(datt)
    dh8, dl8 = split(jnp.broadcast_to(datt, (8, ch)))
    ph, plow = split(proj_ref[...])
    pg_ref[...] = jnp.zeros(pg_ref.shape, F32)
    pg_ref[:, 0:ch] = (dot_nn(dh8, ph) + dot_nn(dh8, plow) + dot_nn(dl8, ph)) * (1.0 / area)
    grad_ref[0:ch, :] = m2
    grad_ref[ch : 2 * ch, 0:ch] = scale * m1
    grad_ref[ch : 2 * ch, ch : 2 * ch] = branch * m3 * attention
    grad_ref[2 * ch : 3 * ch, 0:ch] = dcol * pooled
    dscale = jnp.sum(down_ref[...] * m1, axis=1, keepdims=True)
    dbranch = jnp.sum(squeeze_ref[...] * attention * m3, axis=1, keepdims=True)
    row_at = lax.broadcasted_iota(jnp.int32, (ch, ch), 0)
    vectors = jnp.where(row_at == 0, datt, jnp.where(row_at == 1, to_row(dbranch), jnp.where(row_at == 2, to_row(dscale), 0.0)))
    grad_ref[2 * ch : 3 * ch, ch : 2 * ch] = vectors


def conv_back_kernel(
    width,
    view_ref,
    dkeep_ref,
    dsend_ref,
    pg_ref,
    conv_ref,
    doubled_ref,
    edge_ref,
    band_ref,
    up_ref,
    down_ref,
    exp_ref,
    k_ref,
    dn_ref,
    dnup_ref,
    dndown_ref,
    grad_ref,
    kt_ref,
    dgate_ref,
    bg_ref,
    gk_ref,
    pgcol_ref,
):
    rows, wide, padded = conv_ref.shape
    ch = wide // 2
    half = rows // 2
    view = view_ref[0]
    kernel_columns(k_ref, kt_ref)
    pgcol_ref[...] = jnp.broadcast_to(to_column(pg_ref[0:1, 0:ch]), pgcol_ref.shape)
    for k in range(half):
        dgate_ref[half * view + k] = dkeep_ref[k]
        dgate_ref[half * (1 - view) + k] = dsend_ref[k]
    keep = lane_mask((8, padded), width)
    lanes = lax.broadcasted_iota(jnp.int32, (8, 128), 1)

    def fold_lanes(x):
        total = x[:, 0:128]
        for t in range(128, padded, 128):
            total = total + x[:, t : t + 128]
        return total

    def group(g, carry):
        lower = pl.multiple_of(g * 8, 8)
        at = pl.ds(lower, 8)
        other = pl.ds(pl.multiple_of(lower + ch, 8), 8)
        shift = pgcol_ref[at, 0:1]
        total = [dgate_ref[h, at, :] + shift for h in range(rows)]
        for own, partner in ((at, other), (other, at)):
            taps = kt_ref[own, :]
            moved = []
            for h in range(rows):
                minus, same, plus = shifted(total[h] * conv_ref[h, partner, :])
                moved.append((plus, same, minus))
            sums = [[None] * 3 for _ in range(3)]
            for r in range(-1, rows + 1):
                if r < 0:
                    feature = edge_ref[0, own, :]
                elif r == rows:
                    feature = edge_ref[1, own, :]
                else:
                    feature = doubled_ref[r, own, :]
                back = None
                for i in range(3):
                    src = r - i + 1
                    if 0 <= src < rows:
                        for j in range(3):
                            term = taps[:, 3 * i + j : 3 * i + j + 1] * moved[src][j]
                            back = term if back is None else back + term
                            part = fold_lanes(feature * moved[src][j])
                            sums[i][j] = part if sums[i][j] is None else sums[i][j] + part
                bg_ref[r + 1, own, :] = jnp.where(keep, back, 0.0)
            packed = jnp.zeros((8, 128), F32)
            for i in range(3):
                for j in range(3):
                    packed = jnp.where(lanes == 3 * i + j, jnp.sum(sums[i][j], axis=1, keepdims=True), packed)
            gk_ref[own, :] = packed
        return carry

    lax.fori_loop(0, ch // 8, group, 0)
    weight = left_lanes(exp_ref[...])
    acc = None
    for r in range(rows + 2):
        source = up_ref[...] if r == 0 else down_ref[...] if r == rows + 1 else band_ref[r - 1]
        back = bg_ref[r]
        term = outer_pixels(normed_of(source)[0], back)
        acc = term if acc is None else acc + term
        value = dot_nn(weight, right_rows(back))
        if r == 0:
            dnup_ref[...] = value
        elif r == rows + 1:
            dndown_ref[...] = value
        else:
            dn_ref[r - 1] = value
    grad_ref[0:ch, :] = fold(acc)
    grad_ref[ch : ch + 16, :] = gk_ref[...].T[0:16, :]


def place_rows(o_ref, row, value):
    o_ref[:, row, :] = value[:, 0 : o_ref.shape[2]]


def front_back_kernel(view_ref, dn_ref, above_ref, below_ref, band_ref, keep_ref, send_ref, o_ref, scratch_ref):
    rows = dn_ref.shape[0]
    half = rows // 2
    view = view_ref[0]
    for k in range(half):
        scratch_ref[half * view + k] = keep_ref[k]
        scratch_ref[half * (1 - view) + k] = send_ref[k]
    for h in range(rows):
        dn = dn_ref[h]
        if h == 0:
            dn = dn + above_ref[...]
        if h == rows - 1:
            dn = dn + below_ref[...]
        normed, spread = normed_of(band_ref[h])
        place_rows(o_ref, h, scratch_ref[h] + norm_back(dn, normed, spread))


def assemble_kernel(view_ref, keep_ref, send_ref, o_ref, scratch_ref):
    half = keep_ref.shape[0]
    view = view_ref[0]
    for k in range(half):
        scratch_ref[half * view + k] = keep_ref[k]
        scratch_ref[half * (1 - view) + k] = send_ref[k]
    for h in range(2 * half):
        place_rows(o_ref, h, scratch_ref[h])


def finish_kernel(factor, a_ref, b_ref, c_ref, up_ref, down_ref, squeeze_ref, pool_ref, bias_ref, branch_ref, scale_ref, q_ref, v_ref, s_ref, exp_ref, k_ref):
    ch = q_ref.shape[0]
    q_ref[...] = a_ref[0:ch, 0:ch] * factor
    v_ref[...] = a_ref[0:ch, ch : 2 * ch] * factor
    s_ref[...] = a_ref[ch : ch + 1, 0:ch] * factor
    up_ref[...] = b_ref[0:ch, :] * factor
    down_ref[...] = b_ref[ch : 2 * ch, 0:ch] * factor
    squeeze_ref[...] = b_ref[ch : 2 * ch, ch : 2 * ch] * factor
    pool_ref[...] = b_ref[2 * ch : 3 * ch, 0:ch] * factor
    bias_ref[...] = b_ref[2 * ch : 2 * ch + 1, ch : 2 * ch] * factor
    branch_ref[...] = b_ref[2 * ch + 1 : 2 * ch + 2, ch : 2 * ch] * factor
    scale_ref[...] = b_ref[2 * ch + 2 : 2 * ch + 3, ch : 2 * ch] * factor
    exp_ref[...] = c_ref[0:ch, :] * factor
    for i in range(3):
        k_ref[i] = c_ref[ch + 3 * i : ch + 3 * i + 3, :] * factor


def call(kernel, outs, *args, scalars=0, scratch=(), name=None, cost=None):
    smem = pl.BlockSpec(memory_space=pltpu.SMEM)
    vmem = pl.BlockSpec(memory_space=pltpu.VMEM)
    shapes = tuple(jax.ShapeDtypeStruct(s, F32) for s in outs)
    return pl.pallas_call(
        kernel,
        out_shape=shapes,
        in_specs=[smem] * scalars + [vmem] * (len(args) - scalars),
        out_specs=(vmem,) * len(shapes),
        scratch_shapes=list(scratch),
        compiler_params=pltpu.CompilerParams(vmem_limit_bytes=28 * MIB),
        name=name,
        cost_estimate=cost,
    )(*args)


def swap(x, axis, mask):
    return lax.ppermute(x, axis, [(i, i ^ mask) for i in range(lax.axis_size(axis))])


def sum_over(x, *axes):
    for axis in axes:
        size = lax.axis_size(axis)
        if size & (size - 1):
            x = lax.psum(x, axis)
            continue
        mask = 1
        while mask < size:
            x = x + swap(x, axis, mask)
            mask *= 2
    return x


def per_device(
    frames_in,
    cotangent,
    expand_in,
    conv_kernel,
    pool_proj,
    pool_bias,
    squeeze_out,
    branch_scale,
    ffn_expand,
    ffn_shrink,
    ffn_scale,
    query_proj,
    value_proj,
    cross_scale,
):
    _, frames, ch, rows, width = frames_in.shape
    assert frames == 1 and rows % 2 == 0
    half = rows // 2
    wide = 2 * ch
    padded = -(-width // 128) * 128
    bands = lax.axis_size("row")
    area = rows * bands * width
    factor = (2 * frames * lax.axis_size("dp") * area) ** (-0.5)
    view = lax.axis_index("view").astype(jnp.int32).reshape(1)
    keep_base, send_base = half * view, half * (1 - view)
    part, full = (half, ch, padded), (rows, ch, padded)
    row = (ch, padded)
    exp_t, up_t = expand_in.T, ffn_expand.T
    k_rows = jnp.transpose(conv_kernel, (1, 2, 0))
    bias, branch, scale = (x.reshape(1, ch) for x in (pool_bias, branch_scale, ffn_scale))
    vm = lambda *shape: pltpu.VMEM(shape, F32)

    band, first, last, pack = call(
        start_kernel,
        [full, row, row, (ch + 8, wide)],
        frames_in[0, 0],
        query_proj[0],
        value_proj[0],
        cross_scale,
        name="start",
    )
    up_pairs = [(i, i + 1) for i in range(bands - 1)]
    down_pairs = [(i + 1, i) for i in range(bands - 1)]
    above = lax.ppermute(last, "row", up_pairs)
    below = lax.ppermute(first, "row", down_pairs)
    pack_other = swap(pack, "view", 1)
    doubled, conv_part, cot_send, cot_keep = call(
        conv_own_kernel,
        [(rows, wide, padded)] * 2 + [part] * 2,
        view,
        band,
        exp_t,
        k_rows,
        cotangent[0, 0],
        scalars=1,
        scratch=[vm(wide, wide), vm(rows, ch, padded)],
        name="conv_own",
    )
    cot_other = swap(cot_send, "view", 1)
    conv, edge, gating, pool = call(
        functools.partial(conv_edge_kernel, width),
        [(rows, wide, padded), (2, wide, padded), full, (8, wide)],
        conv_part,
        doubled,
        above,
        below,
        exp_t,
        k_rows,
        scratch=[vm(wide, wide)],
        name="conv_edge",
    )
    pool = sum_over(pool, "row")
    weights = (pool, pool_proj, bias, squeeze_out, branch, up_t, ffn_shrink, scale)

    def tail(base, name):
        return call(
            functools.partial(tail_kernel, area),
            [part, part, (half, wide, padded)],
            base,
            band,
            gating,
            *weights,
            scalars=1,
            name=name,
        )

    hid_send, one_send, expanded_send = tail(send_base, "tail_send")
    hid_other = swap(hid_send, "view", 1)
    hid_keep, one_keep, expanded_keep = tail(keep_base, "tail_keep")
    out_keep, out_send, dh_keep, dh_send, grad_own, grad_other = call(
        functools.partial(attend_kernel, width),
        [part] * 4 + [(ch + 8, wide)] * 2,
        hid_keep,
        hid_other,
        cot_keep,
        cot_other,
        pack,
        pack_other,
        scratch=[vm(padded, padded), pltpu.VMEM((padded, padded), BF16), pltpu.VMEM((padded, padded), BF16)],
        name="attend",
    )
    dh_back = swap(dh_send, "view", 1)
    out_back = swap(out_send, "view", 1)
    grad_a = grad_own + swap(grad_other, "view", 1)
    dgate_keep, done_keep, acc = call(
        functools.partial(tail_back_kernel, area, False),
        [part, part, (wide, 8 * ch)],
        keep_base,
        dh_keep,
        one_keep,
        expanded_keep,
        gating,
        *weights,
        scalars=1,
        name="tail_back_keep",
    )
    dgate_send, done_send, pool_grad, grad_b = call(
        lambda base, dh, one, ex, gate, w0, w1, w2, w3, w4, w5, w6, w7, acc, dg, dn, pg, gr: tail_back_kernel(
            area, True, base, dh, one, ex, gate, w0, w1, w2, w3, w4, w5, w6, w7, acc, None, None, dg, dn, pg, gr
        ),
        [part, part, (8, wide), (3 * ch, wide)],
        send_base,
        dh_back,
        one_send,
        expanded_send,
        gating,
        *weights,
        acc,
        scalars=1,
        name="tail_back_send",
    )
    pool_grad = sum_over(pool_grad, "row")
    grad_a = sum_over(grad_a, "dp", "row")
    grad_b = sum_over(grad_b, "dp", "view", "row")
    (output,) = call(
        assemble_kernel,
        [(ch, rows, width)],
        view,
        out_keep,
        out_back,
        scalars=1,
        scratch=[vm(rows, ch, padded)],
        name="assemble",
    )
    dn, dn_up, dn_down, grad_c = call(
        functools.partial(conv_back_kernel, width),
        [full, row, row, (ch + 16, wide)],
        view,
        dgate_keep,
        dgate_send,
        pool_grad,
        conv,
        doubled,
        edge,
        band,
        above,
        below,
        exp_t,
        k_rows,
        scalars=1,
        scratch=[vm(wide, wide), vm(rows, ch, padded), vm(rows + 2, wide, padded), vm(wide, wide), vm(ch, wide)],
        name="conv_back",
    )
    from_above = lax.ppermute(dn_down, "row", up_pairs)
    from_below = lax.ppermute(dn_up, "row", down_pairs)
    grad_c = sum_over(grad_c, "dp", "view", "row")
    (frames_grad,) = call(
        front_back_kernel,
        [(ch, rows, width)],
        view,
        dn,
        from_above,
        from_below,
        band,
        done_keep,
        done_send,
        scalars=1,
        scratch=[vm(rows, ch, padded)],
        name="front_back",
    )
    g_up, g_down, g_squeeze, g_pool, g_bias, g_branch, g_scale, g_q, g_v, g_s, g_exp, g_k = call(
        functools.partial(finish_kernel, factor),
        [(ch, wide), (ch, ch), (ch, ch), (ch, ch), (1, ch), (1, ch), (1, ch), (ch, ch), (ch, ch), (1, ch), (ch, wide), (3, 3, wide)],
        grad_a,
        grad_b,
        grad_c,
        name="finish",
    )
    return (
        output[None, None],
        frames_grad[None, None],
        g_exp.T,
        jnp.transpose(g_k, (2, 0, 1)),
        g_pool,
        g_bias.reshape(ch),
        g_squeeze,
        g_branch.reshape(ch),
        g_up.T,
        g_down,
        g_scale.reshape(ch),
        g_q[None],
        g_v[None],
        g_s,
    )


def solution(mesh):
    image = P("view", "dp", None, "row", None)
    owned = (P("view", None, None), P("view", None, None), P("view", None))
    return jax.shard_map(
        per_device,
        mesh=mesh,
        in_specs=(image, image) + (P(),) * 9 + owned,
        out_specs=(image, image) + (P(),) * 9 + owned,
        check_vma=False,
    )
```

```python
import functools

import jax
import jax.numpy as jnp
from jax import lax
from jax.experimental import pallas as pl
from jax.experimental.pallas import tpu as pltpu
from jax.sharding import PartitionSpec as P


epsilon = 1e-06
F32 = jnp.float32
BF16 = jnp.bfloat16
MIB = 1 << 20
UNROLL = 2


def split(x):
    high = x.astype(BF16)
    return high, (x - high.astype(F32)).astype(BF16)


def stack_rows(*parts):
    return jnp.concatenate(parts, axis=0)


def left_rows(w):
    h, l = split(w)
    return stack_rows(h, h, l)


def right_rows(x):
    h, l = split(x)
    return stack_rows(h, l, h)


def left_lanes(w):
    h, l = split(w)
    return jnp.concatenate([h, h, l], axis=1)


def dot_nn(a, b):
    return lax.dot_general(a, b, (((1,), (0,)), ((), ())), preferred_element_type=F32)


def dot_tn(a, b):
    return lax.dot_general(a, b, (((0,), (0,)), ((), ())), preferred_element_type=F32)


def dot_nt(a, b):
    return lax.dot_general(a, b, (((1,), (1,)), ((), ())), preferred_element_type=F32)


def outer_pixels(a, b):
    return dot_nt(stack_rows(*split(a)), stack_rows(*split(b)))


def fold(acc):
    m, n = acc.shape[0] // 2, acc.shape[1] // 2
    return acc[:m, :n] + acc[:m, n:] + acc[m:, :n]


def channel_mean(x):
    return jnp.sum(x, axis=0, keepdims=True) * (1.0 / x.shape[0])


def normed_of(x):
    center = x - channel_mean(x)
    scale = 1.0 / jnp.sqrt(channel_mean(center * center) + epsilon)
    return center * scale, scale


def norm_back(grad, normed, scale):
    return scale * (grad - channel_mean(grad) - normed * channel_mean(grad * normed))


def eye(n):
    rows = lax.broadcasted_iota(jnp.int32, (n, n), 0)
    return (rows == lax.broadcasted_iota(jnp.int32, (n, n), 1)).astype(F32)


def to_column(row):
    return jnp.sum(eye(row.shape[1]) * row, axis=1, keepdims=True)


def to_row(column):
    return jnp.sum(eye(column.shape[0]) * column, axis=0, keepdims=True)


def lane_mask(shape, width):
    return lax.broadcasted_iota(jnp.int32, shape, len(shape) - 1) < width


def relayout(x_ref, o_ref):
    rows, width = o_ref.shape[0], x_ref.shape[2]
    padded = o_ref.shape[2]
    for h in range(rows):
        o_ref[h, :, 0:width] = x_ref[:, h, :]
        if padded > width:
            o_ref[h, :, width:padded] = jnp.zeros((o_ref.shape[1], padded - width), F32)


def pack_square(o_ref, base, left, right, row):
    ch = left.shape[0]
    lines = 2 * ch * ch // o_ref.shape[1]
    span = 2 * ch
    o_ref[base : base + lines + 8, :] = jnp.zeros((lines + 8, o_ref.shape[1]), F32)
    for t in range(ch // lines):
        at = slice(t * lines, (t + 1) * lines)
        o_ref[base : base + lines, t * span : t * span + ch] = left[at]
        o_ref[base : base + lines, t * span + ch : (t + 1) * span] = right[at]
    o_ref[base + lines : base + lines + 8, 0:ch] = jnp.broadcast_to(row, (8, ch))


def unpack_square(x_ref, base, ch):
    lines = 2 * ch * ch // x_ref.shape[1]
    span = 2 * ch
    wide = jnp.concatenate([x_ref[base : base + lines, t * span : (t + 1) * span] for t in range(ch // lines)], axis=0)
    return wide[:, :ch], wide[:, ch:], x_ref[base + lines : base + lines + 1, 0:ch]


def start_kernel(
    view_ref,
    core_ref,
    x_hbm,
    cot_hbm,
    q_hbm,
    v_hbm,
    s_hbm,
    band_ref,
    first_ref,
    last_ref,
    keep_ref,
    send_ref,
    x_ref,
    cot_ref,
    q_ref,
    v_ref,
    s_ref,
    scratch_ref,
    sems,
):
    pairs = ((x_hbm, x_ref), (cot_hbm, cot_ref), (q_hbm, q_ref), (v_hbm, v_ref), (s_hbm, s_ref))
    copies = [pltpu.make_async_copy(src, dst, sems.at[i]) for i, (src, dst) in enumerate(pairs)]
    for copy in copies:
        copy.start()
    half, ch, _ = keep_ref.shape
    view = view_ref[0]
    copies[0].wait()
    relayout(x_ref, band_ref)
    first_ref[...] = band_ref[0]
    last_ref[...] = band_ref[2 * half - 1]
    for copy in copies[1:]:
        copy.wait()
    relayout(cot_ref, scratch_ref)
    for k in range(half):
        keep_ref[k] = scratch_ref[half * view + k]
        send_ref[k * ch : (k + 1) * ch, :] = scratch_ref[half * (1 - view) + k]
    pack_square(send_ref, half * ch, q_ref[...], v_ref[...], s_ref[...])


def kernel_columns(k_ref, kt_ref):
    tall = k_ref.shape[2]
    rows = lax.broadcasted_iota(jnp.int32, (tall, tall), 0)
    mat = jnp.zeros((tall, tall), F32)
    for i in range(3):
        for j in range(3):
            mat = jnp.where(rows == 3 * i + j, k_ref[i, j : j + 1, :], mat)
    kt_ref[...] = mat.T


def shifted(x):
    n = x.shape[1]
    return pltpu.roll(x, 1, 1), x, pltpu.roll(x, n - 1, 1)


def conv_own_kernel(width, band_ref, exp_ref, k_ref, doubled_ref, conv_ref, gating_ref, pool_ref, taps_ref):
    rows, ch, padded = band_ref.shape
    kernel_columns(k_ref, taps_ref)
    weight = left_rows(exp_ref[...])
    for h in range(rows):
        doubled_ref[h] = dot_tn(weight, right_rows(normed_of(band_ref[h])[0]))
    keep = lane_mask((8, padded), width)

    def group(g, carry):
        lower = pl.multiple_of(g * 8, 8)
        halves = []
        for offset in (0, ch):
            at = pl.ds(pl.multiple_of(lower + offset, 8), 8)
            taps = taps_ref[at, :]
            moved = [shifted(doubled_ref[h, at, :]) for h in range(rows)]
            out = []
            for h in range(rows):
                total = None
                for i in range(3):
                    src = h + i - 1
                    if 0 <= src < rows:
                        for j in range(3):
                            term = taps[:, 3 * i + j : 3 * i + j + 1] * moved[src][j]
                            total = term if total is None else total + term
                total = jnp.where(keep, total, 0.0)
                conv_ref[h, at, :] = total
                out.append(total)
            halves.append(out)
        at = pl.ds(lower, 8)
        pooled = jnp.zeros((8, padded), F32)
        for h in range(1, rows - 1):
            gate = halves[0][h] * halves[1][h]
            gating_ref[h, at, :] = gate
            pooled = pooled + gate
        pool_ref[at, :] = pooled
        return carry

    lax.fori_loop(0, ch // 8, group, 0, unroll=UNROLL)


def conv_edge_kernel(
    width, conv_in, gating_in, pool_in, taps_ref, up_ref, down_ref, exp_ref, conv_ref, gating_ref, edge_ref, pool_ref, sums_ref
):
    rows, wide, padded = conv_ref.shape
    ch = wide // 2
    weight = left_rows(exp_ref[...])
    edge_ref[0] = dot_tn(weight, right_rows(normed_of(up_ref[...])[0]))
    edge_ref[1] = dot_tn(weight, right_rows(normed_of(down_ref[...])[0]))
    keep = lane_mask((8, padded), width)

    def group(g, carry):
        lower = pl.multiple_of(g * 8, 8)
        gates = [None, None]
        for offset in (0, ch):
            at = pl.ds(pl.multiple_of(lower + offset, 8), 8)
            taps = taps_ref[at, :]
            for side, (h, tap) in enumerate(((0, 0), (rows - 1, 6))):
                moved = shifted(edge_ref[side, at, :])
                total = conv_in[h, at, :]
                for j in range(3):
                    total = total + jnp.where(keep, taps[:, tap + j : tap + j + 1] * moved[j], 0.0)
                conv_ref[h, at, :] = total
                gates[side] = total if gates[side] is None else gates[side] * total
        at = pl.ds(lower, 8)
        gating_ref[0, at, :] = gates[0]
        gating_ref[rows - 1, at, :] = gates[1]
        pooled = pool_in[at, :] + gates[0] + gates[1]
        sums_ref[at, :] = jnp.broadcast_to(jnp.sum(pooled, axis=1, keepdims=True), (8, sums_ref.shape[1]))
        return carry

    lax.fori_loop(0, ch // 8, group, 0, unroll=UNROLL)
    pool_ref[...] = jnp.zeros(pool_ref.shape, F32)
    pool_ref[:, 0:ch] = jnp.broadcast_to(to_row(sums_ref[:, 0:1]), (8, ch))


def total_of(refs):
    total = refs[0][...]
    for ref in refs[1:]:
        total = total + ref[...]
    return total


def base_of(view_ref, half, kept):
    return half * view_ref[0] if kept else half * (1 - view_ref[0])


def attention_of(pool_refs, proj_ref, bias_ref, area):
    ch = proj_ref.shape[0]
    pooled = total_of(pool_refs)[:, 0:ch] * (1.0 / area)
    ph, plow = split(pooled)
    wh, wl = split(proj_ref[...])
    product = dot_nt(ph, wh) + dot_nt(ph, wl) + dot_nt(plow, wh)
    return pooled[0:1], product[0:1] + bias_ref[...]


def tail_kernel(area, kept, parts, view_ref, band_ref, gating_ref, *refs):
    pool_refs, refs = refs[:parts], refs[parts:]
    proj_ref, bias_ref, squeeze_ref, branch_ref, up_ref, down_ref, scale_ref, hidden_ref, one_ref, expanded_ref = refs
    half, ch, _ = hidden_ref.shape
    _, attention = attention_of(pool_refs, proj_ref, bias_ref, area)
    squeeze = left_lanes(to_column(branch_ref[...]) * squeeze_ref[...] * attention)
    up = left_rows(up_ref[...])
    down = left_lanes(to_column(scale_ref[...]) * down_ref[...])
    base = base_of(view_ref, half, kept)
    for k in range(half):
        one = band_ref[base + k] + dot_nn(squeeze, right_rows(gating_ref[base + k]))
        one_ref[k] = one
        expanded = dot_tn(up, right_rows(normed_of(one)[0]))
        expanded_ref[k] = expanded
        hidden_ref[k] = one + dot_nn(down, right_rows(expanded[:ch] * expanded[ch:]))


def attend_kernel(
    width,
    hid0_ref,
    hid1_ref,
    cot0_ref,
    q_ref,
    v_ref,
    s_ref,
    other_ref,
    out0_ref,
    out1_ref,
    dh0_ref,
    dh1_ref,
    grad0_ref,
    grad1_ref,
    e_ref,
    eh_ref,
    el_ref,
):
    half, ch, padded = hid0_ref.shape
    block = 128
    inv = ch ** (-0.5)
    mask = lane_mask((1, padded), width)
    hids = (hid0_ref, hid1_ref)
    q_other, v_other, s_other = unpack_square(other_ref, half * ch, ch)
    wq, wv = (q_ref[...], q_other), (v_ref[...], v_other)
    scale = [to_column(x) for x in (s_ref[...], s_other)]
    lq, lv = [left_lanes(w) for w in wq], [left_lanes(w) for w in wv]
    lqt, lvt = [left_rows(w) for w in wq], [left_rows(w) for w in wv]
    acc_q, acc_v, acc_s = [None, None], [None, None], [None, None]

    def add(acc, s, value):
        acc[s] = value if acc[s] is None else acc[s] + value

    for k in range(half):
        h = [ref[k] for ref in hids]
        u = [cot0_ref[k], other_ref[k * ch : (k + 1) * ch, :]]
        norms = [normed_of(x) for x in h]
        q = [dot_nn(lq[s], right_rows(norms[s][0])) for s in range(2)]
        v = [dot_nn(lv[s], right_rows(h[s])) for s in range(2)]
        qh, ql = zip(*[split(q[0] * inv), split(q[1])])
        vh, vl = zip(*[split(x) for x in v])
        left = stack_rows(qh[0], qh[0], ql[0])
        right = stack_rows(qh[1], ql[1], qh[1])
        col_sum = jnp.zeros((1, padded), F32)
        for b in range(0, padded, block):
            scores = dot_tn(left[:, b : b + block], right)
            weights = jnp.where(mask, jnp.exp(scores), 0.0)
            if b + block > width:
                rows_at = lax.broadcasted_iota(jnp.int32, (block, 1), 0) + b
                weights = jnp.where(rows_at < width, weights, 0.0)
            eh, el = split(weights)
            e_ref[b : b + block, :] = weights
            eh_ref[b : b + block, :] = eh
            el_ref[b : b + block, :] = el
            col_sum = col_sum + jnp.sum(weights, axis=0, keepdims=True)
        b_inv = jnp.where(mask, 1.0 / jnp.where(mask, col_sum, 1.0), 0.0)
        g = [scale[s] * u[s] for s in range(2)]
        bg = g[1] * b_inv
        bgh, bgl = split(bg)
        ones = jnp.ones((16, padded), BF16)
        first = dot_nt(stack_rows(vh[1], vl[1], bgh, bgl, ones), eh_ref[...])
        second = dot_nt(stack_rows(vh[1], bgh, ones), el_ref[...])
        row_sum = first[4 * ch : 4 * ch + 1] + second[2 * ch : 2 * ch + 1]
        a_inv = jnp.where(mask, 1.0 / jnp.where(mask, row_sum, 1.0), 0.0)
        carried0 = (first[0:ch] + first[ch : 2 * ch] + second[0:ch]) * a_inv
        dv0 = first[2 * ch : 3 * ch] + first[3 * ch : 4 * ch] + second[ch : 2 * ch]
        ag = g[0] * a_inv
        agh, agl = split(ag)
        first = dot_nn(stack_rows(vh[0], vl[0], agh, agl), eh_ref[...])
        second = dot_nn(stack_rows(vh[0], agh), el_ref[...])
        carried1 = (first[0:ch] + first[ch : 2 * ch] + second[0:ch]) * b_inv
        dv1 = first[2 * ch : 3 * ch] + first[3 * ch : 4 * ch] + second[ch : 2 * ch]
        out0_ref[k] = h[0] + scale[0] * carried0
        out1_ref[k] = h[1] + scale[1] * carried1
        d0 = jnp.sum(ag * carried0, axis=0, keepdims=True)
        d1 = jnp.sum(bg * carried1, axis=0, keepdims=True)
        d0h, d0l = split(d0)
        row_at = lax.broadcasted_iota(jnp.int32, (16, padded), 0)
        extra = jnp.where(row_at == 0, d0h.astype(F32), jnp.where(row_at == 1, d0l.astype(F32), 0.0)).astype(BF16)
        left = stack_rows(agh, vh[0], agh, vh[0], agl, vl[0], extra)
        right = stack_rows(vh[1], bgh, vl[1], bgl, vh[1], bgh, -ones)
        for b in range(0, padded, block):
            inner = dot_tn(left[:, b : b + block], right) - d1
            dsh, dsl = split(e_ref[b : b + block, :] * inner)
            eh_ref[b : b + block, :] = dsh
            el_ref[b : b + block, :] = dsl
        first = dot_nt(stack_rows(qh[1], ql[1]), eh_ref[...])
        dq0 = (first[0:ch] + first[ch : 2 * ch] + dot_nt(qh[1], el_ref[...])) * inv
        first = dot_nn(stack_rows(qh[0], ql[0]), eh_ref[...])
        dq1 = first[0:ch] + first[ch : 2 * ch] + dot_nn(qh[0], el_ref[...])
        dq, dv, carried = (dq0, dq1), (dv0, dv1), (carried0, carried1)
        for s, ref in enumerate((dh0_ref, dh1_ref)):
            normed, spread = norms[s]
            dn = dot_tn(lqt[s], right_rows(dq[s]))
            ref[k] = u[s] + norm_back(dn, normed, spread) + dot_tn(lvt[s], right_rows(dv[s]))
            add(acc_q, s, outer_pixels(dq[s], normed))
            add(acc_v, s, outer_pixels(dv[s], h[s]))
            add(acc_s, s, u[s] * carried[s])
    for s, ref in enumerate((grad0_ref, grad1_ref)):
        ref[0:ch, 0:ch] = fold(acc_q[s])
        ref[0:ch, ch : 2 * ch] = fold(acc_v[s])
        ref[ch : ref.shape[0], :] = jnp.zeros((ref.shape[0] - ch, 2 * ch), F32)
        ref[ch : ch + 1, 0:ch] = to_row(jnp.sum(acc_s[s], axis=1, keepdims=True))


def tail_back_kernel(area, final, parts, view_ref, dh_ref, one_ref, expanded_ref, gating_ref, *refs):
    pool_refs, refs = refs[:parts], refs[parts:]
    proj_ref, bias_ref, squeeze_ref, branch_ref, up_ref, down_ref, scale_ref = refs[:7]
    refs = refs[7:]
    half, ch, _ = dh_ref.shape
    base = base_of(view_ref, half, not final)
    pooled, attention = attention_of(pool_refs, proj_ref, bias_ref, area)
    branch, scale = to_column(branch_ref[...]), to_column(scale_ref[...])
    mixed = branch * squeeze_ref[...]
    squeeze = left_rows(mixed * attention)
    up = left_lanes(up_ref[...])
    down = left_rows(scale * down_ref[...])
    if final:
        acc_in, dgate_ref, done_ref, pg_ref, grad_ref = refs
    else:
        dgate_ref, done_ref, acc_ref = refs
    acc1 = acc2 = acc3 = None
    for k in range(half):
        dh, one, expanded = dh_ref[k], one_ref[k], expanded_ref[k]
        lower, upper = expanded[:ch], expanded[ch:]
        normed, spread = normed_of(one)
        term1 = outer_pixels(dh, lower * upper)
        dprod = dot_tn(down, right_rows(dh))
        dexp = stack_rows(dprod * upper, dprod * lower)
        term2 = outer_pixels(normed, dexp)
        dn = dot_nn(up, right_rows(dexp))
        done = dh + norm_back(dn, normed, spread)
        done_ref[k] = done
        term3 = outer_pixels(done, gating_ref[base + k])
        dgate_ref[k] = dot_tn(squeeze, right_rows(done))
        acc1 = term1 if acc1 is None else acc1 + term1
        acc2 = term2 if acc2 is None else acc2 + term2
        acc3 = term3 if acc3 is None else acc3 + term3
    if not final:
        acc_ref[:, 0 : 2 * ch] = acc1
        acc_ref[:, 2 * ch : 6 * ch] = acc2
        acc_ref[:, 6 * ch : 8 * ch] = acc3
        return
    m1 = fold(acc1 + acc_in[:, 0 : 2 * ch])
    m2 = fold(acc2 + acc_in[:, 2 * ch : 6 * ch])
    m3 = fold(acc3 + acc_in[:, 6 * ch : 8 * ch])
    datt = jnp.sum(mixed * m3, axis=0, keepdims=True)
    dcol = to_column(datt)
    dh8, dl8 = split(jnp.broadcast_to(datt, (8, ch)))
    ph, plow = split(proj_ref[...])
    pg_ref[...] = jnp.zeros(pg_ref.shape, F32)
    pg_ref[:, 0:ch] = (dot_nn(dh8, ph) + dot_nn(dh8, plow) + dot_nn(dl8, ph)) * (1.0 / area)
    grad_ref[0:ch, :] = m2
    grad_ref[ch : 2 * ch, 0:ch] = scale * m1
    grad_ref[ch : 2 * ch, ch : 2 * ch] = branch * m3 * attention
    grad_ref[2 * ch : 3 * ch, 0:ch] = dcol * pooled
    dscale = jnp.sum(down_ref[...] * m1, axis=1, keepdims=True)
    dbranch = jnp.sum(squeeze_ref[...] * attention * m3, axis=1, keepdims=True)
    row_at = lax.broadcasted_iota(jnp.int32, (ch, ch), 0)
    vectors = jnp.where(row_at == 0, datt, jnp.where(row_at == 1, to_row(dbranch), jnp.where(row_at == 2, to_row(dscale), 0.0)))
    grad_ref[2 * ch : 3 * ch, ch : 2 * ch] = vectors


def conv_back_kernel(width, parts, view_ref, core_ref, *refs):
    conv_back_body(width, view_ref, core_ref, refs[:parts], *refs[parts:])


def conv_back_body(
    width,
    view_ref,
    core_ref,
    pg_refs,
    dkeep_ref,
    dsend_ref,
    conv_ref,
    doubled_ref,
    edge_ref,
    band_ref,
    up_ref,
    down_ref,
    exp_ref,
    kt_ref,
    own_ref,
    other_ref,
    gradb_ref,
    dn_ref,
    dnup_ref,
    dndown_ref,
    mine_ref,
    theirs_ref,
    all_ref,
    dgate_ref,
    bg_ref,
    gk_ref,
    pgcol_ref,
):
    rows, wide, padded = conv_ref.shape
    ch = wide // 2
    half = rows // 2
    view = view_ref[0]
    pgcol_ref[...] = jnp.broadcast_to(to_column(total_of(pg_refs)[0:1, 0:ch]), pgcol_ref.shape)
    for k in range(half):
        dgate_ref[half * view + k] = dkeep_ref[k]
        dgate_ref[half * (1 - view) + k] = dsend_ref[k]
    keep = lane_mask((8, padded), width)
    lanes = lax.broadcasted_iota(jnp.int32, (8, 128), 1)

    def fold_lanes(x):
        total = x[:, 0:128]
        for t in range(128, padded, 128):
            total = total + x[:, t : t + 128]
        return total

    def group(g, carry):
        lower = pl.multiple_of(g * 8, 8)
        at = pl.ds(lower, 8)
        other = pl.ds(pl.multiple_of(lower + ch, 8), 8)
        shift = pgcol_ref[at, 0:1]
        total = [dgate_ref[h, at, :] + shift for h in range(rows)]
        for own, partner in ((at, other), (other, at)):
            taps = kt_ref[own, :]
            moved = []
            for h in range(rows):
                minus, same, plus = shifted(total[h] * conv_ref[h, partner, :])
                moved.append((plus, same, minus))
            sums = [[None] * 3 for _ in range(3)]
            for r in range(-1, rows + 1):
                if r < 0:
                    feature = edge_ref[0, own, :]
                elif r == rows:
                    feature = edge_ref[1, own, :]
                else:
                    feature = doubled_ref[r, own, :]
                back = None
                for i in range(3):
                    src = r - i + 1
                    if 0 <= src < rows:
                        for j in range(3):
                            term = taps[:, 3 * i + j : 3 * i + j + 1] * moved[src][j]
                            back = term if back is None else back + term
                            part = fold_lanes(feature * moved[src][j])
                            sums[i][j] = part if sums[i][j] is None else sums[i][j] + part
                bg_ref[r + 1, own, :] = jnp.where(keep, back, 0.0)
            packed = jnp.zeros((8, 128), F32)
            for i in range(3):
                for j in range(3):
                    packed = jnp.where(lanes == 3 * i + j, jnp.sum(sums[i][j], axis=1, keepdims=True), packed)
            gk_ref[own, :] = packed
        return carry

    lax.fori_loop(0, ch // 8, group, 0, unroll=UNROLL)
    weight = left_lanes(exp_ref[...])
    acc = None
    for r in range(rows + 2):
        source = up_ref[...] if r == 0 else down_ref[...] if r == rows + 1 else band_ref[r - 1]
        back = bg_ref[r]
        term = outer_pixels(normed_of(source)[0], back)
        acc = term if acc is None else acc + term
        value = dot_nn(weight, right_rows(back))
        if r == 0:
            dnup_ref[...] = value
        elif r == rows + 1:
            dndown_ref[...] = value
        else:
            dn_ref[r - 1] = value
    at = gradb_ref.shape[0]
    all_ref[0:at, :] = gradb_ref[...]
    all_ref[at : at + ch, :] = fold(acc)
    all_ref[at + ch : at + ch + 16, :] = gk_ref[...].T[0:16, :]
    core = core_ref[0]
    place = 0
    for ref in (all_ref, own_ref, other_ref):
        lines = ref.shape[0] // 2
        at = slice(place, place + lines)
        mine_ref[at, :] = ref[pl.ds(pl.multiple_of(lines * core, 8), lines), :]
        theirs_ref[at, :] = ref[pl.ds(pl.multiple_of(lines * (1 - core), 8), lines), :]
        place += lines


def place_rows(o_ref, row, value):
    o_ref[:, row, :] = value[:, 0 : o_ref.shape[2]]


def front_back_kernel(view_ref, dn_ref, above_ref, below_ref, band_ref, keep_ref, send_ref, o_ref, scratch_ref):
    rows = dn_ref.shape[0]
    half = rows // 2
    view = view_ref[0]
    for k in range(half):
        scratch_ref[half * view + k] = keep_ref[k]
        scratch_ref[half * (1 - view) + k] = send_ref[k]
    for h in range(rows):
        dn = dn_ref[h]
        if h == 0:
            dn = dn + above_ref[...]
        if h == rows - 1:
            dn = dn + below_ref[...]
        normed, spread = normed_of(band_ref[h])
        place_rows(o_ref, h, scratch_ref[h] + norm_back(dn, normed, spread))


def assemble_kernel(view_ref, keep_ref, send_ref, o_ref, scratch_ref):
    half = keep_ref.shape[0]
    view = view_ref[0]
    for k in range(half):
        scratch_ref[half * view + k] = keep_ref[k]
        scratch_ref[half * (1 - view) + k] = send_ref[k]
    for h in range(2 * half):
        place_rows(o_ref, h, scratch_ref[h])


def finish_kernel(
    factor,
    core_ref,
    mine_ref,
    theirs_ref,
    up_ref,
    down_ref,
    squeeze_ref,
    pool_ref,
    bias_ref,
    branch_ref,
    scale_ref,
    exp_ref,
    k_ref,
    q_ref,
    v_ref,
    s_ref,
    all_ref,
    own_ref,
):
    ch = q_ref.shape[0]
    core = core_ref[0]
    place = 0
    for ref in (all_ref, own_ref):
        lines = ref.shape[0] // 2
        at = slice(place, place + lines)
        ref[pl.ds(pl.multiple_of(lines * core, 8), lines), :] = mine_ref[at, :] * factor
        ref[pl.ds(pl.multiple_of(lines * (1 - core), 8), lines), :] = theirs_ref[at, :] * factor
        place += lines
    up_ref[...] = all_ref[0:ch, :]
    down_ref[...] = all_ref[ch : 2 * ch, 0:ch]
    squeeze_ref[...] = all_ref[ch : 2 * ch, ch : 2 * ch]
    at = 2 * ch
    pool_ref[...] = all_ref[at : at + ch, 0:ch]
    bias_ref[...] = all_ref[at : at + 1, ch : 2 * ch]
    branch_ref[...] = all_ref[at + 1 : at + 2, ch : 2 * ch]
    scale_ref[...] = all_ref[at + 2 : at + 3, ch : 2 * ch]
    at = at + ch
    exp_ref[...] = all_ref[at : at + ch, :]
    at = at + ch
    for i in range(3):
        k_ref[i] = all_ref[at + 3 * i : at + 3 * i + 3, :]
    q_ref[...] = own_ref[0:ch, 0:ch]
    v_ref[...] = own_ref[0:ch, ch : 2 * ch]
    s_ref[...] = own_ref[ch : ch + 1, 0:ch]


def add_kernel(mine_ref, other_ref, o_ref):
    o_ref[...] = mine_ref[...] + other_ref[...]


def add_split_kernel(mine_ref, other_ref, keep_ref, send_ref):
    total, both = mine_ref.shape[0], keep_ref.shape[0]
    owned = total - both
    keep_ref[...] = mine_ref[0:both, :] + other_ref[0:both, :]
    send_ref[0 : both - owned, :] = keep_ref[0 : both - owned, :]
    send_ref[both - owned : both, :] = mine_ref[both:total, :] + other_ref[both:total, :]


def call(kernel, outs, *args, scalars=0, far=0, scratch=(), aliases=None, limit=12 * MIB):
    smem = pl.BlockSpec(memory_space=pltpu.SMEM)
    vmem = pl.BlockSpec(memory_space=pltpu.VMEM)
    hbm = pl.BlockSpec(memory_space=pltpu.HBM)
    shapes = tuple(jax.ShapeDtypeStruct(s, F32) for s in outs)
    return pl.pallas_call(
        kernel,
        out_shape=shapes,
        in_specs=[smem] * scalars + [hbm] * far + [vmem] * (len(args) - scalars - far),
        out_specs=(vmem,) * len(shapes),
        scratch_shapes=list(scratch),
        compiler_params=pltpu.CompilerParams(vmem_limit_bytes=limit),
        input_output_aliases=aliases or {},
    )(*args)


def swap(x, axis, mask):
    return lax.ppermute(x, axis, [(i, i ^ mask) for i in range(lax.axis_size(axis))])


def add(x, y):
    return call(add_kernel, [x.shape], x, y)[0]


def sum_over(x, axis, first=1):
    size, mask = lax.axis_size(axis), first
    if size & (size - 1):
        raise ValueError("axis size")
    while mask < size:
        x = add(x, swap(x, axis, mask))
        mask *= 2
    return x


def parts_over(x, axis):
    if lax.axis_size(axis) > 4:
        return (sum_over(x, axis),)
    return (x,) + tuple(swap(x, axis, mask) for mask in range(1, lax.axis_size(axis)))


def per_device(
    frames_in,
    cotangent,
    expand_in,
    conv_kernel,
    pool_proj,
    pool_bias,
    squeeze_out,
    branch_scale,
    ffn_expand,
    ffn_shrink,
    ffn_scale,
    query_proj,
    value_proj,
    cross_scale,
):
    _, frames, ch, rows, width = frames_in.shape
    assert frames == 1 and rows % 2 == 0
    half = rows // 2
    wide = 2 * ch
    padded = -(-width // 128) * 128
    bands = lax.axis_size("row")
    area = rows * bands * width
    factor = (2 * frames * lax.axis_size("dp") * area) ** (-0.5)
    view = lax.axis_index("view").astype(jnp.int32).reshape(1)
    core = (lax.axis_index("dp").astype(jnp.int32) & 1).reshape(1)
    part, full = (half, ch, padded), (rows, ch, padded)
    row = (ch, padded)
    exp_t, up_t = expand_in.T, ffn_expand.T
    k_rows = jnp.transpose(conv_kernel, (1, 2, 0))
    bias, branch, scale = (x.reshape(1, ch) for x in (pool_bias, branch_scale, ffn_scale))
    vm = lambda *shape: pltpu.VMEM(shape, F32)

    lines = half * ch + wide * ch // padded + 8
    query, value = query_proj[0], value_proj[0]
    image = vm(ch, rows, width)
    band, first, last, cot_keep, pack = call(
        start_kernel,
        [full, row, row, part, (lines, padded)],
        view,
        core,
        frames_in[0, 0],
        cotangent[0, 0],
        query,
        value,
        cross_scale,
        scalars=2,
        far=5,
        scratch=[image, image, vm(ch, ch), vm(ch, ch), vm(1, ch), vm(rows, ch, padded), pltpu.SemaphoreType.DMA((5,))],
        limit=67043328 - 4 * padded * (rows * ch + 2 * ch + half * ch + lines) * 17 // 16,
    )
    up_pairs = [(i, i + 1) for i in range(bands - 1)]
    down_pairs = [(i + 1, i) for i in range(bands - 1)]
    above = lax.ppermute(last, "row", up_pairs)
    below = lax.ppermute(first, "row", down_pairs)
    other = swap(pack, "view", 1)
    doubled, conv, gating, pool, taps = call(
        functools.partial(conv_own_kernel, width),
        [(rows, wide, padded)] * 2 + [full, row, (wide, wide)],
        band,
        exp_t,
        k_rows,
    )
    conv, gating, edge, pool = call(
        functools.partial(conv_edge_kernel, width),
        [(rows, wide, padded), full, (2, wide, padded), (8, wide)],
        conv,
        gating,
        pool,
        taps,
        above,
        below,
        exp_t,
        scratch=[vm(ch, 128)],
        aliases={0: 0, 1: 1},
    )
    pools = parts_over(pool, "row")
    parts = len(pools)
    weights = pools + (pool_proj, bias, squeeze_out, branch, up_t, ffn_shrink, scale)

    def tail(kept):
        return call(
            functools.partial(tail_kernel, area, kept, parts),
            [part, part, (half, wide, padded)],
            view,
            band,
            gating,
            *weights,
            scalars=1,
        )

    hid_send, one_send, expanded_send = tail(False)
    hid_other = swap(hid_send, "view", 1)
    hid_keep, one_keep, expanded_keep = tail(True)
    out_keep, out_send, dh_keep, dh_send, grad_own, grad_other = call(
        functools.partial(attend_kernel, width),
        [part, part, part, part, (ch + 16, wide), (ch + 16, wide)],
        hid_keep,
        hid_other,
        cot_keep,
        query,
        value,
        cross_scale,
        other,
        scratch=[vm(padded, padded), pltpu.VMEM((padded, padded), BF16), pltpu.VMEM((padded, padded), BF16)],
    )
    dh_back = swap(dh_send, "view", 1)
    out_back = swap(out_send, "view", 1)
    dgate_keep, done_keep, acc = call(
        functools.partial(tail_back_kernel, area, False, parts),
        [part, part, (wide, 8 * ch)],
        view,
        dh_keep,
        one_keep,
        expanded_keep,
        gating,
        *weights,
        scalars=1,
    )
    dgate_send, done_send, pool_grad, grad_b = call(
        functools.partial(tail_back_kernel, area, True, parts),
        [part, part, (8, wide), (3 * ch, wide)],
        view,
        dh_back,
        one_send,
        expanded_send,
        gating,
        *weights,
        acc,
        scalars=1,
    )
    pool_grads = parts_over(pool_grad, "row")
    (output,) = call(
        assemble_kernel, [(ch, rows, width)], view, out_keep, out_back, scalars=1, scratch=[vm(rows, ch, padded)]
    )
    shared_lines, owned_lines = 4 * ch + 16, ch + 16
    piece = shared_lines // 2 + owned_lines
    dn, dn_up, dn_down, mine, theirs = call(
        functools.partial(conv_back_kernel, width, len(pool_grads)),
        [full, row, row, (piece, wide), (piece, wide)],
        view,
        core,
        *pool_grads,
        dgate_keep,
        dgate_send,
        conv,
        doubled,
        edge,
        band,
        above,
        below,
        exp_t,
        taps,
        grad_own,
        grad_other,
        grad_b,
        scalars=2,
        scratch=[vm(shared_lines, wide), vm(rows, ch, padded), vm(rows + 2, wide, padded), vm(wide, wide), vm(ch, wide)],
    )
    from_above = lax.ppermute(dn_down, "row", up_pairs)
    from_below = lax.ppermute(dn_up, "row", down_pairs)
    both = (shared_lines + owned_lines) // 2
    mine, send = call(add_split_kernel, [(both, wide)] * 2, mine, swap(theirs, "dp", 1))
    mine = add(mine, swap(send, "view", 1))
    mine = sum_over(mine, "dp", 2)
    mine = sum_over(mine, "row")
    theirs = swap(mine, "dp", 1)
    (frames_grad,) = call(
        front_back_kernel,
        [(ch, rows, width)],
        view,
        dn,
        from_above,
        from_below,
        band,
        done_keep,
        done_send,
        scalars=1,
        scratch=[vm(rows, ch, padded)],
    )
    square, line = (ch, ch), (1, ch)
    g_up, g_down, g_squeeze, g_pool, g_bias, g_branch, g_scale, g_exp, g_k, g_q, g_v, g_s = call(
        functools.partial(finish_kernel, factor),
        [(ch, wide), square, square, square, line, line, line, (ch, wide), (3, 3, wide), square, square, line],
        core,
        mine,
        theirs,
        scalars=1,
        scratch=[vm(shared_lines, wide), vm(owned_lines, wide)],
    )
    return (
        output[None, None],
        frames_grad[None, None],
        g_exp.T,
        jnp.transpose(g_k, (2, 0, 1)),
        g_pool,
        g_bias.reshape(ch),
        g_squeeze,
        g_branch.reshape(ch),
        g_up.T,
        g_down,
        g_scale.reshape(ch),
        g_q[None],
        g_v[None],
        g_s,
    )


def solution(mesh):
    image = P("view", "dp", None, "row", None)
    owned = (P("view", None, None), P("view", None, None), P("view", None))

    return jax.shard_map(
        per_device,
        mesh=mesh,
        in_specs=(image, image) + (P(),) * 9 + owned,
        out_specs=(image, image) + (P(),) * 9 + owned,
        check_vma=False,
    )
```

```python
import functools

import jax
import jax.numpy as jnp
from jax import lax
from jax.experimental import pallas as pl
from jax.experimental.pallas import tpu as pltpu
from jax.sharding import PartitionSpec as P


epsilon = 1e-06
F32 = jnp.float32
BF16 = jnp.bfloat16
MIB = 1 << 20


def split(x):
    high = x.astype(BF16)
    return high, (x - high.astype(F32)).astype(BF16)


def stack_rows(*parts):
    return jnp.concatenate(parts, axis=0)


def left_rows(w):
    h, l = split(w)
    return stack_rows(h, h, l)


def right_rows(x):
    h, l = split(x)
    return stack_rows(h, l, h)


def left_lanes(w):
    h, l = split(w)
    return jnp.concatenate([h, h, l], axis=1)


def dot_nn(a, b):
    return lax.dot_general(a, b, (((1,), (0,)), ((), ())), preferred_element_type=F32)


def dot_tn(a, b):
    return lax.dot_general(a, b, (((0,), (0,)), ((), ())), preferred_element_type=F32)


def dot_nt(a, b):
    return lax.dot_general(a, b, (((1,), (1,)), ((), ())), preferred_element_type=F32)


def outer_pixels(a, b):
    return dot_nt(stack_rows(*split(a)), stack_rows(*split(b)))


def fold(acc):
    m, n = acc.shape[0] // 2, acc.shape[1] // 2
    return acc[:m, :n] + acc[:m, n:] + acc[m:, :n]


def channel_mean(x):
    return jnp.sum(x, axis=0, keepdims=True) * (1.0 / x.shape[0])


def normed_of(x):
    center = x - channel_mean(x)
    scale = 1.0 / jnp.sqrt(channel_mean(center * center) + epsilon)
    return center * scale, scale


def norm_back(grad, normed, scale):
    return scale * (grad - channel_mean(grad) - normed * channel_mean(grad * normed))


def eye(n):
    rows = lax.broadcasted_iota(jnp.int32, (n, n), 0)
    return (rows == lax.broadcasted_iota(jnp.int32, (n, n), 1)).astype(F32)


def to_column(row):
    return jnp.sum(eye(row.shape[1]) * row, axis=1, keepdims=True)


def to_row(column):
    return jnp.sum(eye(column.shape[0]) * column, axis=0, keepdims=True)


def lane_mask(shape, width):
    return lax.broadcasted_iota(jnp.int32, shape, len(shape) - 1) < width


def relayout(x_ref, o_ref):
    rows, width = o_ref.shape[0], x_ref.shape[2]
    padded = o_ref.shape[2]
    for h in range(rows):
        o_ref[h, :, 0:width] = x_ref[:, h, :]
        if padded > width:
            o_ref[h, :, width:padded] = jnp.zeros((o_ref.shape[1], padded - width), F32)


def pack_square(o_ref, base, left, right, row):
    ch = left.shape[0]
    lines = 2 * ch * ch // o_ref.shape[1]
    span = 2 * ch
    o_ref[base : base + lines + 8, :] = jnp.zeros((lines + 8, o_ref.shape[1]), F32)
    for t in range(ch // lines):
        at = slice(t * lines, (t + 1) * lines)
        o_ref[base : base + lines, t * span : t * span + ch] = left[at]
        o_ref[base : base + lines, t * span + ch : (t + 1) * span] = right[at]
    o_ref[base + lines : base + lines + 8, 0:ch] = jnp.broadcast_to(row, (8, ch))


def unpack_square(x_ref, base, ch):
    lines = 2 * ch * ch // x_ref.shape[1]
    span = 2 * ch
    wide = jnp.concatenate([x_ref[base : base + lines, t * span : (t + 1) * span] for t in range(ch // lines)], axis=0)
    return wide[:, :ch], wide[:, ch:], x_ref[base + lines : base + lines + 1, 0:ch]


def start_kernel(view_ref, core_ref, odd_ref, slot_ref, x_ref, band_ref, first_ref, second_ref):
    relayout(x_ref, band_ref)
    end = band_ref.shape[0] - 1
    first_ref[...] = band_ref[end * (1 - odd_ref[0])]
    second_ref[...] = band_ref[end * odd_ref[0]]


def pack_kernel(count, view_ref, *refs):
    fars, (cot_ref, keep_ref, send_ref), refs = refs[:count], refs[count : count + 3], refs[count + 3 :]
    nears, (scratch_ref, sems) = refs[:count], refs[count:]
    copies = [pltpu.make_async_copy(src, dst, sems.at[i]) for i, (src, dst) in enumerate(zip(fars, nears))]
    for copy in copies:
        copy.start()
    half, ch, _ = keep_ref.shape
    view = view_ref[0]
    relayout(cot_ref, scratch_ref)
    for k in range(half):
        keep_ref[k] = scratch_ref[half * view + k]
        send_ref[k * ch : (k + 1) * ch, :] = scratch_ref[half * (1 - view) + k]
    for copy in copies:
        copy.wait()
    q_ref, v_ref, s_ref = nears[:3]
    pack_square(send_ref, half * ch, q_ref[...], v_ref[...], s_ref[...])


def kernel_columns(k_ref, kt_ref):
    tall = k_ref.shape[2]
    rows = lax.broadcasted_iota(jnp.int32, (tall, tall), 0)
    mat = jnp.zeros((tall, tall), F32)
    for i in range(3):
        for j in range(3):
            mat = jnp.where(rows == 3 * i + j, k_ref[i, j : j + 1, :], mat)
    kt_ref[...] = mat.T


def shifted(x):
    n = x.shape[1]
    return pltpu.roll(x, 1, 1), x, pltpu.roll(x, n - 1, 1)


def conv_own_kernel(width, band_ref, exp_ref, k_ref, doubled_ref, conv_ref, gating_ref, pool_ref, taps_ref):
    rows, ch, padded = band_ref.shape
    kernel_columns(k_ref, taps_ref)
    weight = left_rows(exp_ref[...])
    for h in range(rows):
        doubled_ref[h] = dot_tn(weight, right_rows(normed_of(band_ref[h])[0]))
    keep = lane_mask((8, padded), width)

    def group(g, carry):
        lower = pl.multiple_of(g * 8, 8)
        halves = []
        for offset in (0, ch):
            at = pl.ds(pl.multiple_of(lower + offset, 8), 8)
            taps = taps_ref[at, :]
            moved = [shifted(doubled_ref[h, at, :]) for h in range(rows)]
            out = []
            for h in range(rows):
                total = None
                for i in range(3):
                    src = h + i - 1
                    if 0 <= src < rows:
                        for j in range(3):
                            term = taps[:, 3 * i + j : 3 * i + j + 1] * moved[src][j]
                            total = term if total is None else total + term
                total = jnp.where(keep, total, 0.0)
                conv_ref[h, at, :] = total
                out.append(total)
            halves.append(out)
        at = pl.ds(lower, 8)
        pooled = jnp.zeros((8, padded), F32)
        for h in range(1, rows - 1):
            gate = halves[0][h] * halves[1][h]
            gating_ref[h, at, :] = gate
            pooled = pooled + gate
        pool_ref[at, :] = pooled
        return carry

    lax.fori_loop(0, ch // 8, group, 0, unroll=True)


def conv_edge_kernel(
    width,
    odd_ref,
    conv_in,
    gating_in,
    pool_in,
    taps_ref,
    first_ref,
    second_ref,
    exp_ref,
    conv_ref,
    gating_ref,
    edge_ref,
    halo_ref,
    pool_ref,
    sums_ref,
):
    rows, wide, padded = conv_ref.shape
    ch = wide // 2
    weight = left_rows(exp_ref[...])
    odd = odd_ref[0]
    for side, choice in enumerate((odd == 1, odd == 0)):
        normed = normed_of(jnp.where(choice, first_ref[...], second_ref[...]))[0]
        halo_ref[side] = normed
        edge_ref[side] = dot_tn(weight, right_rows(normed))
    keep = lane_mask((8, padded), width)

    def group(g, carry):
        lower = pl.multiple_of(g * 8, 8)
        gates = [None, None]
        for offset in (0, ch):
            at = pl.ds(pl.multiple_of(lower + offset, 8), 8)
            taps = taps_ref[at, :]
            for side, (h, tap) in enumerate(((0, 0), (rows - 1, 6))):
                moved = shifted(edge_ref[side, at, :])
                total = conv_in[h, at, :]
                for j in range(3):
                    total = total + jnp.where(keep, taps[:, tap + j : tap + j + 1] * moved[j], 0.0)
                conv_ref[h, at, :] = total
                gates[side] = total if gates[side] is None else gates[side] * total
        at = pl.ds(lower, 8)
        gating_ref[0, at, :] = gates[0]
        gating_ref[rows - 1, at, :] = gates[1]
        pooled = pool_in[at, :] + gates[0] + gates[1]
        sums_ref[at, :] = jnp.broadcast_to(jnp.sum(pooled, axis=1, keepdims=True), (8, sums_ref.shape[1]))
        return carry

    lax.fori_loop(0, ch // 8, group, 0, unroll=True)
    pool_ref[...] = jnp.zeros(pool_ref.shape, F32)
    pool_ref[:, 0:ch] = jnp.broadcast_to(to_row(sums_ref[:, 0:1]), (8, ch))


def total_of(refs):
    total = refs[0][...]
    for ref in refs[1:]:
        total = total + ref[...]
    return total


def base_of(view_ref, half, kept):
    return half * view_ref[0] if kept else half * (1 - view_ref[0])


def attention_of(pool_refs, proj_ref, bias_ref, area):
    ch = proj_ref.shape[0]
    pooled = total_of(pool_refs)[:, 0:ch] * (1.0 / area)
    ph, plow = split(pooled)
    wh, wl = split(proj_ref[...])
    product = dot_nt(ph, wh) + dot_nt(ph, wl) + dot_nt(plow, wh)
    return pooled[0:1], product[0:1] + bias_ref[...]


def tail_kernel(area, kept, picks, parts, view_ref, band_ref, gating_ref, *refs):
    pool_refs, refs = refs[:parts], refs[parts:]
    proj_ref, bias_ref, squeeze_ref, branch_ref, up_ref, down_ref, scale_ref, one_ref, expanded_ref = refs[:9]
    hidden_refs = refs[9:]
    ch = squeeze_ref.shape[0]
    _, attention = attention_of(pool_refs, proj_ref, bias_ref, area)
    squeeze = left_lanes(to_column(branch_ref[...]) * squeeze_ref[...] * attention)
    up = left_rows(up_ref[...])
    down = left_lanes(to_column(scale_ref[...]) * down_ref[...])
    base = base_of(view_ref, band_ref.shape[0] // 2, kept)
    for n, k in enumerate(picks):
        one = band_ref[base + k] + dot_nn(squeeze, right_rows(gating_ref[base + k]))
        one_ref[n] = one
        expanded = dot_tn(up, right_rows(normed_of(one)[0]))
        expanded_ref[n] = expanded
        hidden_refs[n][...] = one + dot_nn(down, right_rows(expanded[:ch] * expanded[ch:]))


def attend_kernel(width, k, hid0_ref, hid1_ref, cot0_ref, q_ref, v_ref, s_ref, other_ref, *refs):
    if k:
        before_ref, refs = refs[0], refs[1:]
    out0_ref, out1_ref, dh0_ref, dh1_ref, grad0_ref, grad1_ref, e_ref, eh_ref, el_ref = refs
    ch, padded = hid0_ref.shape
    half = cot0_ref.shape[0]
    if k:
        out1_ref[0:k] = before_ref[...]
    block = 128
    inv = ch ** (-0.5)
    mask = lane_mask((1, padded), width)
    hids = (hid0_ref, hid1_ref)
    q_other, v_other, s_other = unpack_square(other_ref, half * ch, ch)
    wq, wv = (q_ref[...], q_other), (v_ref[...], v_other)
    scale = [to_column(x) for x in (s_ref[...], s_other)]
    lq, lv = [left_lanes(w) for w in wq], [left_lanes(w) for w in wv]
    lqt, lvt = [left_rows(w) for w in wq], [left_rows(w) for w in wv]
    h = [ref[...] for ref in hids]
    u = [cot0_ref[k], other_ref[k * ch : (k + 1) * ch, :]]
    norms = [normed_of(x) for x in h]
    q = [dot_nn(lq[s], right_rows(norms[s][0])) for s in range(2)]
    v = [dot_nn(lv[s], right_rows(h[s])) for s in range(2)]
    qh, ql = zip(*[split(q[0] * inv), split(q[1])])
    vh, vl = zip(*[split(x) for x in v])
    left = stack_rows(qh[0], qh[0], ql[0])
    right = stack_rows(qh[1], ql[1], qh[1])
    col_sum = jnp.zeros((1, padded), F32)
    for b in range(0, padded, block):
        scores = dot_tn(left[:, b : b + block], right)
        weights = jnp.where(mask, jnp.exp(scores), 0.0)
        if b + block > width:
            rows_at = lax.broadcasted_iota(jnp.int32, (block, 1), 0) + b
            weights = jnp.where(rows_at < width, weights, 0.0)
        eh, el = split(weights)
        e_ref[b : b + block, :] = weights
        eh_ref[b : b + block, :] = eh
        el_ref[b : b + block, :] = el
        col_sum = col_sum + jnp.sum(weights, axis=0, keepdims=True)
    b_inv = jnp.where(mask, 1.0 / jnp.where(mask, col_sum, 1.0), 0.0)
    g = [scale[s] * u[s] for s in range(2)]
    bg = g[1] * b_inv
    bgh, bgl = split(bg)
    ones = jnp.ones((16, padded), BF16)
    first = dot_nt(stack_rows(vh[1], vl[1], bgh, bgl, ones), eh_ref[...])
    second = dot_nt(stack_rows(vh[1], bgh, ones), el_ref[...])
    row_sum = first[4 * ch : 4 * ch + 1] + second[2 * ch : 2 * ch + 1]
    a_inv = jnp.where(mask, 1.0 / jnp.where(mask, row_sum, 1.0), 0.0)
    carried0 = (first[0:ch] + first[ch : 2 * ch] + second[0:ch]) * a_inv
    dv0 = first[2 * ch : 3 * ch] + first[3 * ch : 4 * ch] + second[ch : 2 * ch]
    ag = g[0] * a_inv
    agh, agl = split(ag)
    first = dot_nn(stack_rows(vh[0], vl[0], agh, agl), eh_ref[...])
    second = dot_nn(stack_rows(vh[0], agh), el_ref[...])
    carried1 = (first[0:ch] + first[ch : 2 * ch] + second[0:ch]) * b_inv
    dv1 = first[2 * ch : 3 * ch] + first[3 * ch : 4 * ch] + second[ch : 2 * ch]
    out0_ref[...] = h[0] + scale[0] * carried0
    out1_ref[k] = h[1] + scale[1] * carried1
    d0 = jnp.sum(ag * carried0, axis=0, keepdims=True)
    d1 = jnp.sum(bg * carried1, axis=0, keepdims=True)
    d0h, d0l = split(d0)
    row_at = lax.broadcasted_iota(jnp.int32, (16, padded), 0)
    extra = jnp.where(row_at == 0, d0h.astype(F32), jnp.where(row_at == 1, d0l.astype(F32), 0.0)).astype(BF16)
    left = stack_rows(agh, vh[0], agh, vh[0], agl, vl[0], extra)
    right = stack_rows(vh[1], bgh, vl[1], bgl, vh[1], bgh, -ones)
    for b in range(0, padded, block):
        inner = dot_tn(left[:, b : b + block], right) - d1
        dsh, dsl = split(e_ref[b : b + block, :] * inner)
        eh_ref[b : b + block, :] = dsh
        el_ref[b : b + block, :] = dsl
    first = dot_nt(stack_rows(qh[1], ql[1]), eh_ref[...])
    dq0 = (first[0:ch] + first[ch : 2 * ch] + dot_nt(qh[1], el_ref[...])) * inv
    first = dot_nn(stack_rows(qh[0], ql[0]), eh_ref[...])
    dq1 = first[0:ch] + first[ch : 2 * ch] + dot_nn(qh[0], el_ref[...])
    dq, dv, carried = (dq0, dq1), (dv0, dv1), (carried0, carried1)
    for s, (ref, grad_ref) in enumerate(((dh0_ref, grad0_ref), (dh1_ref, grad1_ref))):
        normed, spread = norms[s]
        dn = dot_tn(lqt[s], right_rows(dq[s]))
        ref[...] = u[s] + norm_back(dn, normed, spread) + dot_tn(lvt[s], right_rows(dv[s]))
        grad_ref[0:ch, 0:ch] = fold(outer_pixels(dq[s], normed))
        grad_ref[0:ch, ch : 2 * ch] = fold(outer_pixels(dv[s], h[s]))
        grad_ref[ch : grad_ref.shape[0], :] = jnp.zeros((grad_ref.shape[0] - ch, 2 * ch), F32)
        grad_ref[ch : ch + 1, 0:ch] = to_row(jnp.sum(u[s] * carried[s], axis=1, keepdims=True))


def tail_back_kernel(area, kept, picks, first, final, parts, view_ref, slot_ref, gating_ref, one_ref, expanded_ref, *refs):
    dh_refs, refs = refs[: len(picks)], refs[len(picks) :]
    pool_refs, refs = refs[:parts], refs[parts:]
    proj_ref, bias_ref, squeeze_ref, branch_ref, up_ref, down_ref, scale_ref = refs[:7]
    refs = refs[7:]
    if not first:
        acc_in, refs = refs[0], refs[1:]
    if final:
        own_ref, dgate_ref, done_ref, pg_ref, grad_ref = refs
    else:
        dgate_ref, done_ref, acc_ref = refs
    ch = squeeze_ref.shape[0]
    base = base_of(view_ref, gating_ref.shape[0] // 2, kept)
    _, attention = attention_of(pool_refs, proj_ref, bias_ref, area)
    branch, scale = to_column(branch_ref[...]), to_column(scale_ref[...])
    mixed = branch * squeeze_ref[...]
    squeeze = left_rows(mixed * attention)
    up = left_lanes(up_ref[...])
    down = left_rows(scale * down_ref[...])
    acc1 = acc2 = acc3 = None
    if not first:
        acc1, acc2, acc3 = acc_in[:, 0 : 2 * ch], acc_in[:, 2 * ch : 6 * ch], acc_in[:, 6 * ch : 8 * ch]
    for n, k in enumerate(picks):
        dh, one, expanded = dh_refs[n][...], one_ref[n], expanded_ref[n]
        lower, upper = expanded[:ch], expanded[ch:]
        normed, spread = normed_of(one)
        term1 = outer_pixels(dh, lower * upper)
        dprod = dot_tn(down, right_rows(dh))
        dexp = stack_rows(dprod * upper, dprod * lower)
        term2 = outer_pixels(normed, dexp)
        dn = dot_nn(up, right_rows(dexp))
        done = dh + norm_back(dn, normed, spread)
        done_ref[n] = done
        term3 = outer_pixels(done, gating_ref[base + k])
        dgate_ref[n] = dot_tn(squeeze, right_rows(done))
        acc1 = term1 if acc1 is None else acc1 + term1
        acc2 = term2 if acc2 is None else acc2 + term2
        acc3 = term3 if acc3 is None else acc3 + term3
    if not final:
        acc_ref[:, 0 : 2 * ch] = acc1
        acc_ref[:, 2 * ch : 6 * ch] = acc2
        acc_ref[:, 6 * ch : 8 * ch] = acc3
        return
    m1, m2, m3 = fold(acc1), fold(acc2), fold(acc3)
    datt = jnp.sum(mixed * m3, axis=0, keepdims=True)
    dh8, dl8 = split(jnp.broadcast_to(datt, (8, ch)))
    ph, plow = split(proj_ref[...])
    pg_ref[...] = jnp.zeros(pg_ref.shape, F32)
    pg_ref[:, 0:ch] = (dot_nn(dh8, ph) + dot_nn(dh8, plow) + dot_nn(dl8, ph)) * (1.0 / area)
    grad_ref[0:ch, :] = m2
    grad_ref[ch : 2 * ch, 0:ch] = scale * m1
    grad_ref[ch : 2 * ch, ch : 2 * ch] = branch * m3 * attention
    slots = grad_ref.shape[0] - 2 * ch - 8
    here = lax.broadcasted_iota(jnp.int32, (slots, ch), 0) == slot_ref[0]
    at = slice(2 * ch, 2 * ch + slots)
    grad_ref[at, 0:ch] = jnp.where(here, datt, 0.0)
    grad_ref[at, ch : 2 * ch] = jnp.where(here, own_ref[0:1, 0:ch] * (1.0 / area), 0.0)
    at = slice(2 * ch + slots, 2 * ch + slots + 8)
    dscale = jnp.sum(down_ref[...] * m1, axis=1, keepdims=True)
    dbranch = jnp.sum(squeeze_ref[...] * attention * m3, axis=1, keepdims=True)
    grad_ref[at, 0:ch] = jnp.broadcast_to(to_row(dbranch), (8, ch))
    grad_ref[at, ch : 2 * ch] = jnp.broadcast_to(to_row(dscale), (8, ch))


def conv_back_kernel(width, parts, half, view_ref, core_ref, odd_ref, *refs):
    pools, refs = refs[:parts], refs[parts:]
    sends, refs = refs[:half], refs[half:]
    owns, others, refs = refs[:half], refs[half : 2 * half], refs[2 * half :]
    conv_back_body(width, view_ref, core_ref, odd_ref, pools, sends, owns, others, *refs)


def conv_back_body(
    width,
    view_ref,
    core_ref,
    odd_ref,
    pg_refs,
    dsend_refs,
    own_refs,
    other_refs,
    dkeep_ref,
    conv_ref,
    doubled_ref,
    edge_ref,
    band_ref,
    halo_ref,
    exp_ref,
    kt_ref,
    gradb_ref,
    dn_ref,
    first_ref,
    second_ref,
    mine_ref,
    theirs_ref,
    all_ref,
    dgate_ref,
    bg_ref,
    gk_ref,
    pgcol_ref,
    own_ref,
    other_ref,
):
    rows, wide, padded = conv_ref.shape
    ch = wide // 2
    half = rows // 2
    view = view_ref[0]
    pgcol_ref[...] = jnp.broadcast_to(to_column(total_of(pg_refs)[0:1, 0:ch]), pgcol_ref.shape)
    for k in range(half):
        dgate_ref[half * view + k] = dkeep_ref[k]
        dgate_ref[half * (1 - view) + k] = dsend_refs[k][0]
    keep = lane_mask((8, padded), width)
    lanes = lax.broadcasted_iota(jnp.int32, (8, 128), 1)

    def fold_lanes(x):
        total = x[:, 0:128]
        for t in range(128, padded, 128):
            total = total + x[:, t : t + 128]
        return total

    def group(g, carry):
        lower = pl.multiple_of(g * 8, 8)
        at = pl.ds(lower, 8)
        other = pl.ds(pl.multiple_of(lower + ch, 8), 8)
        shift = pgcol_ref[at, 0:1]
        total = [dgate_ref[h, at, :] + shift for h in range(rows)]
        for own, partner in ((at, other), (other, at)):
            taps = kt_ref[own, :]
            moved = []
            for h in range(rows):
                minus, same, plus = shifted(total[h] * conv_ref[h, partner, :])
                moved.append((plus, same, minus))
            sums = [[None] * 3 for _ in range(3)]
            for r in range(-1, rows + 1):
                if r < 0:
                    feature = edge_ref[0, own, :]
                elif r == rows:
                    feature = edge_ref[1, own, :]
                else:
                    feature = doubled_ref[r, own, :]
                back = None
                for i in range(3):
                    src = r - i + 1
                    if 0 <= src < rows:
                        for j in range(3):
                            term = taps[:, 3 * i + j : 3 * i + j + 1] * moved[src][j]
                            back = term if back is None else back + term
                            part = fold_lanes(feature * moved[src][j])
                            sums[i][j] = part if sums[i][j] is None else sums[i][j] + part
                bg_ref[r + 1, own, :] = jnp.where(keep, back, 0.0)
            packed = jnp.zeros((8, 128), F32)
            for i in range(3):
                for j in range(3):
                    packed = jnp.where(lanes == 3 * i + j, jnp.sum(sums[i][j], axis=1, keepdims=True), packed)
            gk_ref[own, :] = packed
        return carry

    lax.fori_loop(0, ch // 8, group, 0, unroll=True)
    weight = left_lanes(exp_ref[...])
    acc = None
    for r in range(rows + 2):
        normed = halo_ref[0] if r == 0 else halo_ref[1] if r == rows + 1 else normed_of(band_ref[r - 1])[0]
        back = bg_ref[r]
        term = outer_pixels(normed, back)
        acc = term if acc is None else acc + term
        value = dot_nn(weight, right_rows(back))
        if r == 0:
            above = value
        elif r == rows + 1:
            below = value
        else:
            dn_ref[r - 1] = value
    odd = odd_ref[0] == 1
    first_ref[...] = jnp.where(odd, above, below)
    second_ref[...] = jnp.where(odd, below, above)
    at = gradb_ref.shape[0]
    all_ref[0:at, :] = gradb_ref[...]
    all_ref[at : at + ch, :] = fold(acc)
    all_ref[at + ch : at + ch + 16, :] = gk_ref[...].T[0:16, :]
    at = at + ch + 16
    if at < all_ref.shape[0]:
        all_ref[at : all_ref.shape[0], :] = jnp.zeros((all_ref.shape[0] - at, wide), F32)
    own_ref[...] = total_of(own_refs)
    other_ref[...] = total_of(other_refs)
    core = core_ref[0]
    place = 0
    for ref in (all_ref, own_ref, other_ref):
        lines = ref.shape[0] // 2
        at = slice(place, place + lines)
        mine_ref[at, :] = ref[pl.ds(pl.multiple_of(lines * core, 8), lines), :]
        theirs_ref[at, :] = ref[pl.ds(pl.multiple_of(lines * (1 - core), 8), lines), :]
        place += lines


def place_rows(o_ref, row, value):
    o_ref[:, row, :] = value[:, 0 : o_ref.shape[2]]


def collect(view_ref, scratch_ref, kept, sent):
    half = scratch_ref.shape[0] // 2
    for k in range(half):
        scratch_ref[base_of(view_ref, half, True) + k] = kept[k]
        scratch_ref[base_of(view_ref, half, False) + k] = sent[k]


def front_back_kernel(half, view_ref, odd_ref, dn_ref, first_ref, second_ref, band_ref, keep_ref, *refs):
    sends, (o_ref, scratch_ref) = refs[:half], refs[half:]
    rows = dn_ref.shape[0]
    collect(view_ref, scratch_ref, keep_ref, [ref[0] for ref in sends])
    for h in range(rows):
        dn = dn_ref[h]
        if h == 0:
            dn = dn + jnp.where(odd_ref[0] == 1, first_ref[...], second_ref[...])
        if h == rows - 1:
            dn = dn + jnp.where(odd_ref[0] == 1, second_ref[...], first_ref[...])
        normed, spread = normed_of(band_ref[h])
        place_rows(o_ref, h, scratch_ref[h] + norm_back(dn, normed, spread))


def assemble_kernel(half, view_ref, sent_ref, *refs):
    keeps, (o_ref, scratch_ref) = refs[:half], refs[half:]
    collect(view_ref, scratch_ref, [ref[...] for ref in keeps], sent_ref)
    for h in range(2 * half):
        place_rows(o_ref, h, scratch_ref[h])


def finish_kernel(
    factor,
    slots,
    core_ref,
    mine_ref,
    theirs_ref,
    up_ref,
    down_ref,
    squeeze_ref,
    pool_ref,
    bias_ref,
    branch_ref,
    scale_ref,
    exp_ref,
    k_ref,
    q_ref,
    v_ref,
    s_ref,
    all_ref,
    own_ref,
):
    ch = q_ref.shape[0]
    core = core_ref[0]
    place = 0
    for ref in (all_ref, own_ref):
        lines = ref.shape[0] // 2
        at = slice(place, place + lines)
        ref[pl.ds(pl.multiple_of(lines * core, 8), lines), :] = mine_ref[at, :] * factor
        ref[pl.ds(pl.multiple_of(lines * (1 - core), 8), lines), :] = theirs_ref[at, :] * factor
        place += lines
    up_ref[...] = all_ref[0:ch, :]
    down_ref[...] = all_ref[ch : 2 * ch, 0:ch]
    squeeze_ref[...] = all_ref[ch : 2 * ch, ch : 2 * ch]
    at = 2 * ch
    slots = all_ref[at : at + slots, :]
    pool_ref[...] = lax.dot_general(
        slots[:, 0:ch],
        slots[:, ch : 2 * ch] * (1.0 / factor),
        (((0,), (0,)), ((), ())),
        precision=lax.Precision.HIGHEST,
        preferred_element_type=F32,
    )
    bias_ref[...] = jnp.sum(slots[:, 0:ch], axis=0, keepdims=True)
    at = at + slots.shape[0]
    branch_ref[...] = all_ref[at : at + 1, 0:ch]
    scale_ref[...] = all_ref[at : at + 1, ch : 2 * ch]
    at = at + 8
    exp_ref[...] = all_ref[at : at + ch, :]
    at = at + ch
    for i in range(3):
        k_ref[i] = all_ref[at + 3 * i : at + 3 * i + 3, :]
    q_ref[...] = own_ref[0:ch, 0:ch]
    v_ref[...] = own_ref[0:ch, ch : 2 * ch]
    s_ref[...] = own_ref[ch : ch + 1, 0:ch]


def add_kernel(mine_ref, other_ref, o_ref):
    o_ref[...] = mine_ref[...] + other_ref[...]


def add_split_kernel(mine_ref, other_ref, keep_ref, send_ref):
    total, both = mine_ref.shape[0], keep_ref.shape[0]
    owned = total - both
    keep_ref[...] = mine_ref[0:both, :] + other_ref[0:both, :]
    send_ref[0 : both - owned, :] = keep_ref[0 : both - owned, :]
    send_ref[both - owned : both, :] = mine_ref[both:total, :] + other_ref[both:total, :]


def call(kernel, outs, *args, scalars=0, far=0, scratch=(), aliases=None, limit=12 * MIB):
    smem = pl.BlockSpec(memory_space=pltpu.SMEM)
    vmem = pl.BlockSpec(memory_space=pltpu.VMEM)
    hbm = pl.BlockSpec(memory_space=pltpu.HBM)
    shapes = tuple(jax.ShapeDtypeStruct(s, F32) for s in outs)
    return pl.pallas_call(
        kernel,
        out_shape=shapes,
        in_specs=[smem] * scalars + [hbm] * far + [vmem] * (len(args) - scalars - far),
        out_specs=(vmem,) * len(shapes),
        scratch_shapes=list(scratch),
        compiler_params=pltpu.CompilerParams(vmem_limit_bytes=limit),
        input_output_aliases=aliases or {},
    )(*args)


def swap(x, axis, mask):
    return lax.ppermute(x, axis, [(i, i ^ mask) for i in range(lax.axis_size(axis))])


def add(x, y):
    return call(add_kernel, [x.shape], x, y)[0]


def sum_over(x, axis, first=1):
    size, mask = lax.axis_size(axis), first
    if size & (size - 1):
        raise ValueError("axis size")
    while mask < size:
        x = add(x, swap(x, axis, mask))
        mask *= 2
    return x


def parts_over(x, axis):
    if lax.axis_size(axis) > 4:
        return (sum_over(x, axis),)
    return (x,) + tuple(swap(x, axis, mask) for mask in range(1, lax.axis_size(axis)))


def per_device(
    frames_in,
    cotangent,
    expand_in,
    conv_kernel,
    pool_proj,
    pool_bias,
    squeeze_out,
    branch_scale,
    ffn_expand,
    ffn_shrink,
    ffn_scale,
    query_proj,
    value_proj,
    cross_scale,
):
    _, frames, ch, rows, width = frames_in.shape
    assert frames == 1 and rows % 2 == 0
    half = rows // 2
    wide = 2 * ch
    padded = -(-width // 128) * 128
    bands = lax.axis_size("row")
    area = rows * bands * width
    factor = (2 * frames * lax.axis_size("dp") * area) ** (-0.5)
    view = lax.axis_index("view").astype(jnp.int32).reshape(1)
    core = (lax.axis_index("dp").astype(jnp.int32) & 1).reshape(1)
    odd = (lax.axis_index("row").astype(jnp.int32) & 1).reshape(1)
    slot = (2 * lax.axis_index("dp") + lax.axis_index("view")).astype(jnp.int32).reshape(1)
    slots = -(-2 * lax.axis_size("dp") // 8) * 8
    part, full = (half, ch, padded), (rows, ch, padded)
    row = (ch, padded)
    exp_t, up_t = expand_in.T, ffn_expand.T
    k_rows = jnp.transpose(conv_kernel, (1, 2, 0))
    bias, branch, scale = (x.reshape(1, ch) for x in (pool_bias, branch_scale, ffn_scale))
    vm = lambda *shape: pltpu.VMEM(shape, F32)

    lines = half * ch + wide * ch // padded + 8
    query, value = query_proj[0], value_proj[0]
    band, border0, border1 = call(start_kernel, [full, row, row], view, core, odd, slot, frames_in[0, 0], scalars=4)
    pairs = [
        [pair for i in range(begin, bands - 1, 2) for pair in ((i, i + 1), (i + 1, i))] for begin in range(2)
    ]

    def meet(x, turn):
        return lax.ppermute(x, "row", pairs[turn])

    border0 = meet(border0, 0)
    border1 = meet(border1, 1)
    square, line = (ch, ch), (1, ch)
    fars = (query, value, cross_scale, pool_proj, bias, squeeze_out, branch, up_t, ffn_shrink, scale)
    cot_keep, pack, *nears = call(
        functools.partial(pack_kernel, len(fars)),
        [part, (lines, padded)] + [x.shape for x in fars],
        view,
        *(pltpu.with_memory_space_constraint(x, pltpu.HBM) for x in fars),
        cotangent[0, 0],
        scalars=1,
        far=len(fars),
        scratch=[vm(rows, ch, padded), pltpu.SemaphoreType.DMA((len(fars),))],
    )
    query, value, cross, pool_proj, bias, squeeze_out, branch, up_t, ffn_shrink, scale = nears
    other = swap(pack, "view", 1)
    doubled, conv, gating, pool, taps = call(
        functools.partial(conv_own_kernel, width),
        [(rows, wide, padded)] * 2 + [full, row, (wide, wide)],
        band,
        exp_t,
        k_rows,
    )
    conv, gating, edge, halo, pool = call(
        functools.partial(conv_edge_kernel, width),
        [(rows, wide, padded), full, (2, wide, padded), (2, ch, padded), (8, wide)],
        odd,
        conv,
        gating,
        pool,
        taps,
        border0,
        border1,
        exp_t,
        scalars=1,
        scratch=[vm(ch, 128)],
        aliases={1: 0, 2: 1},
    )
    pools = parts_over(pool, "row")
    parts = len(pools)
    weights = pools + (pool_proj, bias, squeeze_out, branch, up_t, ffn_shrink, scale)

    every = range(half)

    def tail(kept, picks):
        count = len(picks)
        one, expanded, *hidden = call(
            functools.partial(tail_kernel, area, kept, picks, parts),
            [(count, ch, padded), (count, wide, padded)] + [row] * count,
            view,
            band,
            gating,
            *weights,
            scalars=1,
        )
        return one, expanded, hidden

    sent, hid_other = [], []
    for k in every:
        one, expanded, (hidden,) = tail(False, (k,))
        sent.append((one, expanded))
        hid_other.append(swap(hidden, "view", 1))
    one_keep, expanded_keep, hid_keep = tail(True, tuple(every))
    out_keep, dh_keep, dh_back, own_grads, other_grads = [], [], [], [], []
    out_send = ()
    for k in every:
        out, out_send, dh, dh_send, own, other_grad = call(
            functools.partial(attend_kernel, width, k),
            [row, (k + 1, ch, padded), row, row, (ch + 16, wide), (ch + 16, wide)],
            hid_keep[k],
            hid_other[k],
            cot_keep,
            query,
            value,
            cross,
            other,
            *((out_send,) if k else ()),
            scratch=[vm(padded, padded), pltpu.VMEM((padded, padded), BF16), pltpu.VMEM((padded, padded), BF16)],
        )
        out_keep.append(out)
        dh_keep.append(dh)
        own_grads.append(own)
        other_grads.append(other_grad)
        dh_back.append(swap(dh_send, "view", 1))
    out_back = swap(out_send, "view", 1)

    def tail_back(kept, picks, final, one, expanded, dh, acc):
        count = len(picks)
        ends = [(8, wide), (2 * ch + slots + 8, wide)] if final else [(wide, 8 * ch)]
        return call(
            functools.partial(tail_back_kernel, area, kept, picks, acc is None, final, parts),
            [(count, ch, padded)] * 2 + ends,
            view,
            slot,
            gating,
            one,
            expanded,
            *dh,
            *weights,
            *(() if acc is None else (acc,)),
            *((pool,) if final else ()),
            scalars=2,
        )

    dgate_keep, done_keep, acc = tail_back(True, tuple(every), False, one_keep, expanded_keep, dh_keep, None)
    dgate_send, done_send = [], []
    for k in every:
        final = k == half - 1
        dgate, done, *rest = tail_back(False, (k,), final, *sent[k], [dh_back[k]], acc)
        acc = rest[0]
        dgate_send.append(dgate)
        done_send.append(done)
    pool_grad, grad_b = rest
    pool_grads = parts_over(pool_grad, "row")
    (output,) = call(
        functools.partial(assemble_kernel, half),
        [(ch, rows, width)],
        view,
        out_back,
        *out_keep,
        scalars=1,
        scratch=[vm(rows, ch, padded)],
    )
    shared_lines = -(-(2 * ch + slots + 8 + ch + 16) // 16) * 16
    owned_lines = ch + 16
    piece = shared_lines // 2 + owned_lines
    dn, border0, border1, mine, theirs = call(
        functools.partial(conv_back_kernel, width, len(pool_grads), half),
        [full, row, row, (piece, wide), (piece, wide)],
        view,
        core,
        odd,
        *pool_grads,
        *dgate_send,
        *own_grads,
        *other_grads,
        dgate_keep,
        conv,
        doubled,
        edge,
        band,
        halo,
        exp_t,
        taps,
        grad_b,
        scalars=3,
        scratch=[vm(shared_lines, wide), vm(rows, ch, padded), vm(rows + 2, wide, padded), vm(wide, wide), vm(ch, wide)]
        + [vm(owned_lines, wide)] * 2,
    )
    border0 = meet(border0, 0)
    border1 = meet(border1, 1)
    both = (shared_lines + owned_lines) // 2
    mine, send = call(add_split_kernel, [(both, wide)] * 2, mine, swap(theirs, "dp", 1))
    mine = add(mine, swap(send, "view", 1))
    mine = sum_over(mine, "dp", 2)
    mine = sum_over(mine, "row")
    theirs = swap(mine, "dp", 1)
    (frames_grad,) = call(
        functools.partial(front_back_kernel, half),
        [(ch, rows, width)],
        view,
        odd,
        dn,
        border0,
        border1,
        band,
        done_keep,
        *done_send,
        scalars=2,
        scratch=[vm(rows, ch, padded)],
    )
    g_up, g_down, g_squeeze, g_pool, g_bias, g_branch, g_scale, g_exp, g_k, g_q, g_v, g_s = call(
        functools.partial(finish_kernel, factor, slots),
        [(ch, wide), square, square, square, line, line, line, (ch, wide), (3, 3, wide), square, square, line],
        core,
        mine,
        theirs,
        scalars=1,
        scratch=[vm(shared_lines, wide), vm(owned_lines, wide)],
    )
    return (
        output[None, None],
        frames_grad[None, None],
        g_exp.T,
        jnp.transpose(g_k, (2, 0, 1)),
        g_pool,
        g_bias.reshape(ch),
        g_squeeze,
        g_branch.reshape(ch),
        g_up.T,
        g_down,
        g_scale.reshape(ch),
        g_q[None],
        g_v[None],
        g_s,
    )


def solution(mesh):
    image = P("view", "dp", None, "row", None)
    owned = (P("view", None, None), P("view", None, None), P("view", None))

    return jax.shard_map(
        per_device,
        mesh=mesh,
        in_specs=(image, image) + (P(),) * 9 + owned,
        out_specs=(image, image) + (P(),) * 9 + owned,
        check_vma=False,
    )
```

```python
import functools

import jax
import jax.numpy as jnp
from jax import lax
from jax.experimental import pallas as pl
from jax.experimental.pallas import tpu as pltpu
from jax.sharding import PartitionSpec as P


epsilon = 1e-06
F32 = jnp.float32
BF16 = jnp.bfloat16
MIB = 1 << 20


def split(x):
    high = x.astype(BF16)
    return high, (x - high.astype(F32)).astype(BF16)


def stack_rows(*parts):
    return jnp.concatenate(parts, axis=0)


def left_rows(w):
    h, l = split(w)
    return stack_rows(h, h, l)


def right_rows(x):
    h, l = split(x)
    return stack_rows(h, l, h)


def left_lanes(w):
    h, l = split(w)
    return jnp.concatenate([h, h, l], axis=1)


def dot_nn(a, b):
    return lax.dot_general(a, b, (((1,), (0,)), ((), ())), preferred_element_type=F32)


def dot_tn(a, b):
    return lax.dot_general(a, b, (((0,), (0,)), ((), ())), preferred_element_type=F32)


def dot_nt(a, b):
    return lax.dot_general(a, b, (((1,), (1,)), ((), ())), preferred_element_type=F32)


def outer_pixels(a, b):
    return dot_nt(stack_rows(*split(a)), stack_rows(*split(b)))


def fold(acc):
    m, n = acc.shape[0] // 2, acc.shape[1] // 2
    return acc[:m, :n] + acc[:m, n:] + acc[m:, :n]


def channel_mean(x):
    return jnp.sum(x, axis=0, keepdims=True) * (1.0 / x.shape[0])


def normed_of(x):
    center = x - channel_mean(x)
    scale = 1.0 / jnp.sqrt(channel_mean(center * center) + epsilon)
    return center * scale, scale


def norm_back(grad, normed, scale):
    return scale * (grad - channel_mean(grad) - normed * channel_mean(grad * normed))


def eye(n):
    rows = lax.broadcasted_iota(jnp.int32, (n, n), 0)
    return (rows == lax.broadcasted_iota(jnp.int32, (n, n), 1)).astype(F32)


def to_column(row):
    return jnp.sum(eye(row.shape[1]) * row, axis=1, keepdims=True)


def to_row(column):
    return jnp.sum(eye(column.shape[0]) * column, axis=0, keepdims=True)


def lane_mask(shape, width):
    return lax.broadcasted_iota(jnp.int32, shape, len(shape) - 1) < width


def relayout(x_ref, o_ref):
    rows, width = o_ref.shape[0], x_ref.shape[2]
    padded = o_ref.shape[2]
    for h in range(rows):
        o_ref[h, :, 0:width] = x_ref[:, h, :]
        if padded > width:
            o_ref[h, :, width:padded] = jnp.zeros((o_ref.shape[1], padded - width), F32)


def pack_square(o_ref, base, left, right, row):
    ch = left.shape[0]
    lines = 2 * ch * ch // o_ref.shape[1]
    span = 2 * ch
    o_ref[base : base + lines + 8, :] = jnp.zeros((lines + 8, o_ref.shape[1]), F32)
    for t in range(ch // lines):
        at = slice(t * lines, (t + 1) * lines)
        o_ref[base : base + lines, t * span : t * span + ch] = left[at]
        o_ref[base : base + lines, t * span + ch : (t + 1) * span] = right[at]
    o_ref[base + lines : base + lines + 8, 0:ch] = jnp.broadcast_to(row, (8, ch))


def unpack_square(x_ref, base, ch):
    lines = 2 * ch * ch // x_ref.shape[1]
    span = 2 * ch
    wide = jnp.concatenate([x_ref[base : base + lines, t * span : (t + 1) * span] for t in range(ch // lines)], axis=0)
    return wide[:, :ch], wide[:, ch:], x_ref[base + lines : base + lines + 1, 0:ch]


def start_kernel(view_ref, core_ref, odd_ref, slot_ref, x_ref, band_ref, first_ref, second_ref):
    relayout(x_ref, band_ref)
    end = band_ref.shape[0] - 1
    first_ref[...] = band_ref[end * (1 - odd_ref[0])]
    second_ref[...] = band_ref[end * odd_ref[0]]


def pack_kernel(count, view_ref, *refs):
    fars, (cot_ref, keep_ref, send_ref), refs = refs[:count], refs[count : count + 3], refs[count + 3 :]
    nears, (scratch_ref, sems) = refs[:count], refs[count:]
    copies = [pltpu.make_async_copy(src, dst, sems.at[i]) for i, (src, dst) in enumerate(zip(fars, nears))]
    for copy in copies:
        copy.start()
    half, ch, _ = keep_ref.shape
    view = view_ref[0]
    relayout(cot_ref, scratch_ref)
    for k in range(half):
        keep_ref[k] = scratch_ref[half * view + k]
        send_ref[k * ch : (k + 1) * ch, :] = scratch_ref[half * (1 - view) + k]
    for copy in copies:
        copy.wait()
    q_ref, v_ref, s_ref = nears[:3]
    pack_square(send_ref, half * ch, q_ref[...], v_ref[...], s_ref[...])


def kernel_columns(k_ref, kt_ref):
    tall = k_ref.shape[2]
    rows = lax.broadcasted_iota(jnp.int32, (tall, tall), 0)
    mat = jnp.zeros((tall, tall), F32)
    for i in range(3):
        for j in range(3):
            mat = jnp.where(rows == 3 * i + j, k_ref[i, j : j + 1, :], mat)
    kt_ref[...] = mat.T


def shifted(x):
    n = x.shape[1]
    return pltpu.roll(x, 1, 1), x, pltpu.roll(x, n - 1, 1)


def conv_own_kernel(width, band_ref, exp_ref, k_ref, doubled_ref, conv_ref, gating_ref, pool_ref, taps_ref):
    rows, ch, padded = band_ref.shape
    kernel_columns(k_ref, taps_ref)
    weight = left_rows(exp_ref[...])
    for h in range(rows):
        doubled_ref[h] = dot_tn(weight, right_rows(normed_of(band_ref[h])[0]))
    keep = lane_mask((8, padded), width)

    def group(g, carry):
        lower = pl.multiple_of(g * 8, 8)
        halves = []
        for offset in (0, ch):
            at = pl.ds(pl.multiple_of(lower + offset, 8), 8)
            taps = taps_ref[at, :]
            moved = [shifted(doubled_ref[h, at, :]) for h in range(rows)]
            out = []
            for h in range(rows):
                total = None
                for i in range(3):
                    src = h + i - 1
                    if 0 <= src < rows:
                        for j in range(3):
                            term = taps[:, 3 * i + j : 3 * i + j + 1] * moved[src][j]
                            total = term if total is None else total + term
                total = jnp.where(keep, total, 0.0)
                conv_ref[h, at, :] = total
                out.append(total)
            halves.append(out)
        at = pl.ds(lower, 8)
        pooled = jnp.zeros((8, padded), F32)
        for h in range(1, rows - 1):
            gate = halves[0][h] * halves[1][h]
            gating_ref[h, at, :] = gate
            pooled = pooled + gate
        pool_ref[at, :] = pooled
        return carry

    lax.fori_loop(0, ch // 8, group, 0, unroll=True)


def conv_edge_kernel(
    width,
    odd_ref,
    conv_in,
    gating_in,
    pool_in,
    taps_ref,
    first_ref,
    second_ref,
    exp_ref,
    conv_ref,
    gating_ref,
    edge_ref,
    halo_ref,
    pool_ref,
    sums_ref,
):
    rows, wide, padded = conv_ref.shape
    ch = wide // 2
    weight = left_rows(exp_ref[...])
    odd = odd_ref[0]
    for side, choice in enumerate((odd == 1, odd == 0)):
        normed = normed_of(jnp.where(choice, first_ref[...], second_ref[...]))[0]
        halo_ref[side] = normed
        edge_ref[side] = dot_tn(weight, right_rows(normed))
    keep = lane_mask((8, padded), width)

    def group(g, carry):
        lower = pl.multiple_of(g * 8, 8)
        gates = [None, None]
        for offset in (0, ch):
            at = pl.ds(pl.multiple_of(lower + offset, 8), 8)
            taps = taps_ref[at, :]
            for side, (h, tap) in enumerate(((0, 0), (rows - 1, 6))):
                moved = shifted(edge_ref[side, at, :])
                total = conv_in[h, at, :]
                for j in range(3):
                    total = total + jnp.where(keep, taps[:, tap + j : tap + j + 1] * moved[j], 0.0)
                conv_ref[h, at, :] = total
                gates[side] = total if gates[side] is None else gates[side] * total
        at = pl.ds(lower, 8)
        gating_ref[0, at, :] = gates[0]
        gating_ref[rows - 1, at, :] = gates[1]
        pooled = pool_in[at, :] + gates[0] + gates[1]
        sums_ref[at, :] = jnp.broadcast_to(jnp.sum(pooled, axis=1, keepdims=True), (8, sums_ref.shape[1]))
        return carry

    lax.fori_loop(0, ch // 8, group, 0, unroll=True)
    pool_ref[...] = jnp.zeros(pool_ref.shape, F32)
    pool_ref[:, 0:ch] = jnp.broadcast_to(to_row(sums_ref[:, 0:1]), (8, ch))


def total_of(refs):
    total = refs[0][...]
    for ref in refs[1:]:
        total = total + ref[...]
    return total


def base_of(view_ref, half, kept):
    return half * view_ref[0] if kept else half * (1 - view_ref[0])


def attention_of(pool_refs, proj_ref, bias_ref, area):
    ch = proj_ref.shape[0]
    pooled = total_of(pool_refs)[:, 0:ch] * (1.0 / area)
    ph, plow = split(pooled)
    wh, wl = split(proj_ref[...])
    product = dot_nt(ph, wh) + dot_nt(ph, wl) + dot_nt(plow, wh)
    return product[0:1] + bias_ref[...]


def tail_kernel(area, kept, picks, parts, view_ref, band_ref, gating_ref, *refs):
    if parts:
        pool_refs, (proj_ref, bias_ref), refs = refs[:parts], refs[parts : parts + 2], refs[parts + 2 :]
    else:
        att_ref, refs = refs[0], refs[1:]
    squeeze_ref, branch_ref, up_ref, down_ref, scale_ref, one_ref, expanded_ref = refs[:7]
    hidden_refs = refs[7 : 7 + len(picks)]
    ch = squeeze_ref.shape[0]
    if parts:
        attention = attention_of(pool_refs, proj_ref, bias_ref, area)
        refs[-1][...] = jnp.broadcast_to(attention, (8, ch))
    else:
        attention = att_ref[0:1, :]
    squeeze = left_lanes(to_column(branch_ref[...]) * squeeze_ref[...] * attention)
    up = left_rows(up_ref[...])
    down = left_lanes(to_column(scale_ref[...]) * down_ref[...])
    base = base_of(view_ref, band_ref.shape[0] // 2, kept)
    for n, k in enumerate(picks):
        one = band_ref[base + k] + dot_nn(squeeze, right_rows(gating_ref[base + k]))
        one_ref[n] = one
        expanded = dot_tn(up, right_rows(normed_of(one)[0]))
        expanded_ref[n] = expanded
        hidden_refs[n][...] = one + dot_nn(down, right_rows(expanded[:ch] * expanded[ch:]))


def attend_kernel(width, k, hid0_ref, hid1_ref, cot0_ref, q_ref, v_ref, s_ref, other_ref, *refs):
    if k:
        before_ref, refs = refs[0], refs[1:]
    out0_ref, out1_ref, dh0_ref, dh1_ref, terms_ref, e_ref, eh_ref, el_ref = refs
    ch, padded = hid0_ref.shape
    half = cot0_ref.shape[0]
    if k:
        out1_ref[0:k] = before_ref[...]
    block = 256
    inv = ch ** (-0.5)
    mask = lane_mask((1, padded), width)
    hids = (hid0_ref, hid1_ref)
    q_other, v_other, s_other = unpack_square(other_ref, half * ch, ch)
    wq, wv = (q_ref[...], q_other), (v_ref[...], v_other)
    scale = [to_column(x) for x in (s_ref[...], s_other)]
    lq, lv = [left_lanes(w) for w in wq], [left_lanes(w) for w in wv]
    lqt, lvt = [left_rows(w) for w in wq], [left_rows(w) for w in wv]
    h = [ref[...] for ref in hids]
    u = [cot0_ref[k], other_ref[k * ch : (k + 1) * ch, :]]
    norms = [normed_of(x) for x in h]
    q = [dot_nn(lq[s], right_rows(norms[s][0])) for s in range(2)]
    v = [dot_nn(lv[s], right_rows(h[s])) for s in range(2)]
    qh, ql = zip(*[split(q[0] * inv), split(q[1])])
    vh, vl = zip(*[split(x) for x in v])
    left = stack_rows(qh[0], qh[0], ql[0])
    right = stack_rows(qh[1], ql[1], qh[1])
    col_sum = jnp.zeros((1, padded), F32)
    for b in range(0, padded, block):
        scores = dot_tn(left[:, b : b + block], right)
        weights = jnp.where(mask, jnp.exp(scores), 0.0)
        if b + block > width:
            rows_at = lax.broadcasted_iota(jnp.int32, (block, 1), 0) + b
            weights = jnp.where(rows_at < width, weights, 0.0)
        eh, el = split(weights)
        e_ref[b : b + block, :] = weights
        eh_ref[b : b + block, :] = eh
        el_ref[b : b + block, :] = el
        col_sum = col_sum + jnp.sum(weights, axis=0, keepdims=True)
    b_inv = jnp.where(mask, 1.0 / jnp.where(mask, col_sum, 1.0), 0.0)
    g = [scale[s] * u[s] for s in range(2)]
    bg = g[1] * b_inv
    bgh, bgl = split(bg)
    ones = jnp.ones((16, padded), BF16)
    first = dot_nt(stack_rows(vh[1], vl[1], bgh, bgl, ones), eh_ref[...])
    second = dot_nt(stack_rows(vh[1], bgh, ones), el_ref[...])
    row_sum = first[4 * ch : 4 * ch + 1] + second[2 * ch : 2 * ch + 1]
    a_inv = jnp.where(mask, 1.0 / jnp.where(mask, row_sum, 1.0), 0.0)
    carried0 = (first[0:ch] + first[ch : 2 * ch] + second[0:ch]) * a_inv
    dv0 = first[2 * ch : 3 * ch] + first[3 * ch : 4 * ch] + second[ch : 2 * ch]
    ag = g[0] * a_inv
    agh, agl = split(ag)
    first = dot_nn(stack_rows(vh[0], vl[0], agh, agl), eh_ref[...])
    second = dot_nn(stack_rows(vh[0], agh), el_ref[...])
    carried1 = (first[0:ch] + first[ch : 2 * ch] + second[0:ch]) * b_inv
    dv1 = first[2 * ch : 3 * ch] + first[3 * ch : 4 * ch] + second[ch : 2 * ch]
    out0_ref[...] = h[0] + scale[0] * carried0
    out1_ref[k] = h[1] + scale[1] * carried1
    d0 = jnp.sum(ag * carried0, axis=0, keepdims=True)
    d1 = jnp.sum(bg * carried1, axis=0, keepdims=True)
    d0h, d0l = split(d0)
    row_at = lax.broadcasted_iota(jnp.int32, (16, padded), 0)
    extra = jnp.where(row_at == 0, d0h.astype(F32), jnp.where(row_at == 1, d0l.astype(F32), 0.0)).astype(BF16)
    left = stack_rows(agh, vh[0], agh, vh[0], agl, vl[0], extra)
    right = stack_rows(vh[1], bgh, vl[1], bgl, vh[1], bgh, -ones)
    for b in range(0, padded, block):
        inner = dot_tn(left[:, b : b + block], right) - d1
        dsh, dsl = split(e_ref[b : b + block, :] * inner)
        eh_ref[b : b + block, :] = dsh
        el_ref[b : b + block, :] = dsl
    first = dot_nt(stack_rows(qh[1], ql[1]), eh_ref[...])
    dq0 = (first[0:ch] + first[ch : 2 * ch] + dot_nt(qh[1], el_ref[...])) * inv
    first = dot_nn(stack_rows(qh[0], ql[0]), eh_ref[...])
    dq1 = first[0:ch] + first[ch : 2 * ch] + dot_nn(qh[0], el_ref[...])
    dq, dv, carried = (dq0, dq1), (dv0, dv1), (carried0, carried1)
    for s, ref in enumerate((dh0_ref, dh1_ref)):
        normed, spread = norms[s]
        dn = dot_tn(lqt[s], right_rows(dq[s]))
        ref[...] = u[s] + norm_back(dn, normed, spread) + dot_tn(lvt[s], right_rows(dv[s]))
        terms_ref[3 * s] = dq[s]
        terms_ref[3 * s + 1] = dv[s]
        terms_ref[3 * s + 2] = u[s] * carried[s]


def attend_grads_kernel(half, *refs):
    terms, hids, grads = refs[:half], (refs[half : 2 * half], refs[2 * half : 3 * half]), refs[3 * half :]
    ch = hids[0][0].shape[0]
    for s, grad_ref in enumerate(grads):
        queries = values = scales = None
        for k in range(half):
            hidden = hids[s][k][...]
            query = outer_pixels(terms[k][3 * s], normed_of(hidden)[0])
            value = outer_pixels(terms[k][3 * s + 1], hidden)
            scale = terms[k][3 * s + 2]
            queries = query if k == 0 else queries + query
            values = value if k == 0 else values + value
            scales = scale if k == 0 else scales + scale
        grad_ref[0:ch, 0:ch] = fold(queries)
        grad_ref[0:ch, ch : 2 * ch] = fold(values)
        grad_ref[ch : grad_ref.shape[0], :] = jnp.zeros((grad_ref.shape[0] - ch, 2 * ch), F32)
        grad_ref[ch : ch + 1, 0:ch] = to_row(jnp.sum(scales, axis=1, keepdims=True))


def tail_back_kernel(area, kept, picks, first, final, view_ref, gating_ref, one_ref, expanded_ref, *refs):
    dh_refs, refs = refs[: len(picks)], refs[len(picks) :]
    att_ref, squeeze_ref, branch_ref, up_ref, down_ref, scale_ref = refs[:6]
    refs = refs[6:]
    if not first:
        acc_in, refs = refs[0], refs[1:]
    if final:
        proj_ref, refs = refs[0], refs[1:]
    dgate_ref, done_ref, acc_ref = refs[:3]
    ch = squeeze_ref.shape[0]
    base = base_of(view_ref, gating_ref.shape[0] // 2, kept)
    attention = att_ref[0:1, :]
    mixed = to_column(branch_ref[...]) * squeeze_ref[...]
    squeeze = left_rows(mixed * attention)
    up = left_lanes(up_ref[...])
    down = left_rows(to_column(scale_ref[...]) * down_ref[...])
    acc1 = acc2 = acc3 = None
    if not first:
        acc1, acc2, acc3 = acc_in[:, 0 : 2 * ch], acc_in[:, 2 * ch : 6 * ch], acc_in[:, 6 * ch : 8 * ch]
    for n, k in enumerate(picks):
        dh, one, expanded = dh_refs[n][...], one_ref[n], expanded_ref[n]
        lower, upper = expanded[:ch], expanded[ch:]
        normed, spread = normed_of(one)
        term1 = outer_pixels(dh, lower * upper)
        dprod = dot_tn(down, right_rows(dh))
        dexp = stack_rows(dprod * upper, dprod * lower)
        term2 = outer_pixels(normed, dexp)
        dn = dot_nn(up, right_rows(dexp))
        done = dh + norm_back(dn, normed, spread)
        done_ref[n] = done
        term3 = outer_pixels(done, gating_ref[base + k])
        dgate_ref[n] = dot_tn(squeeze, right_rows(done))
        acc1 = term1 if acc1 is None else acc1 + term1
        acc2 = term2 if acc2 is None else acc2 + term2
        acc3 = term3 if acc3 is None else acc3 + term3
    acc_ref[:, 0 : 2 * ch] = acc1
    acc_ref[:, 2 * ch : 6 * ch] = acc2
    acc_ref[:, 6 * ch : 8 * ch] = acc3
    if final:
        datt = jnp.sum(mixed * fold(acc3), axis=0, keepdims=True)
        dh8, dl8 = split(jnp.broadcast_to(datt, (8, ch)))
        ph, plow = split(proj_ref[...])
        pg_ref = refs[3]
        pg_ref[...] = jnp.zeros(pg_ref.shape, F32)
        pg_ref[:, 0:ch] = (dot_nn(dh8, ph) + dot_nn(dh8, plow) + dot_nn(dl8, ph)) * (1.0 / area)


def tail_grads_kernel(area, slot_ref, acc_ref, att_ref, squeeze_ref, branch_ref, down_ref, scale_ref, own_ref, grad_ref):
    ch = squeeze_ref.shape[0]
    attention = att_ref[0:1, :]
    branch, scale = to_column(branch_ref[...]), to_column(scale_ref[...])
    m1, m2, m3 = fold(acc_ref[:, 0 : 2 * ch]), fold(acc_ref[:, 2 * ch : 6 * ch]), fold(acc_ref[:, 6 * ch : 8 * ch])
    datt = jnp.sum(branch * squeeze_ref[...] * m3, axis=0, keepdims=True)
    grad_ref[0:ch, :] = m2
    grad_ref[ch : 2 * ch, 0:ch] = scale * m1
    grad_ref[ch : 2 * ch, ch : 2 * ch] = branch * m3 * attention
    slots = grad_ref.shape[0] - 2 * ch - 8
    here = lax.broadcasted_iota(jnp.int32, (slots, ch), 0) == slot_ref[0]
    at = slice(2 * ch, 2 * ch + slots)
    grad_ref[at, 0:ch] = jnp.where(here, datt, 0.0)
    grad_ref[at, ch : 2 * ch] = jnp.where(here, own_ref[0:1, 0:ch] * (1.0 / area), 0.0)
    at = slice(2 * ch + slots, 2 * ch + slots + 8)
    dscale = jnp.sum(down_ref[...] * m1, axis=1, keepdims=True)
    dbranch = jnp.sum(squeeze_ref[...] * attention * m3, axis=1, keepdims=True)
    grad_ref[at, 0:ch] = jnp.broadcast_to(to_row(dbranch), (8, ch))
    grad_ref[at, ch : 2 * ch] = jnp.broadcast_to(to_row(dscale), (8, ch))


def conv_back_kernel(width, parts, half, view_ref, core_ref, odd_ref, *refs):
    pools, refs = refs[:parts], refs[parts:]
    sends, refs = refs[:half], refs[half:]
    conv_back_body(width, view_ref, core_ref, odd_ref, pools, sends, *refs)


def conv_back_body(
    width,
    view_ref,
    core_ref,
    odd_ref,
    pg_refs,
    dsend_refs,
    own_ref,
    other_ref,
    dkeep_ref,
    conv_ref,
    doubled_ref,
    edge_ref,
    band_ref,
    halo_ref,
    exp_ref,
    kt_ref,
    gradb_ref,
    dn_ref,
    first_ref,
    second_ref,
    mine_ref,
    theirs_ref,
    all_ref,
    bg_ref,
    dgate_ref,
    gk_ref,
    pgcol_ref,
):
    rows, wide, padded = conv_ref.shape
    ch = wide // 2
    half = rows // 2
    view = view_ref[0]
    pgcol_ref[...] = jnp.broadcast_to(to_column(total_of(pg_refs)[0:1, 0:ch]), pgcol_ref.shape)
    for k in range(half):
        dgate_ref[half * view + k] = dkeep_ref[k]
        dgate_ref[half * (1 - view) + k] = dsend_refs[k][0]
    keep = lane_mask((8, padded), width)
    lanes = lax.broadcasted_iota(jnp.int32, (8, 128), 1)

    def fold_lanes(x):
        total = x[:, 0:128]
        for t in range(128, padded, 128):
            total = total + x[:, t : t + 128]
        return total

    def group(g, carry):
        lower = pl.multiple_of(g * 8, 8)
        at = pl.ds(lower, 8)
        other = pl.ds(pl.multiple_of(lower + ch, 8), 8)
        shift = pgcol_ref[at, 0:1]
        total = [dgate_ref[h, at, :] + shift for h in range(rows)]
        for own, partner in ((at, other), (other, at)):
            taps = kt_ref[own, :]
            moved = []
            for h in range(rows):
                minus, same, plus = shifted(total[h] * conv_ref[h, partner, :])
                moved.append((plus, same, minus))
            sums = [[None] * 3 for _ in range(3)]
            for r in range(-1, rows + 1):
                if r < 0:
                    feature = edge_ref[0, own, :]
                elif r == rows:
                    feature = edge_ref[1, own, :]
                else:
                    feature = doubled_ref[r, own, :]
                back = None
                for i in range(3):
                    src = r - i + 1
                    if 0 <= src < rows:
                        for j in range(3):
                            term = taps[:, 3 * i + j : 3 * i + j + 1] * moved[src][j]
                            back = term if back is None else back + term
                            part = fold_lanes(feature * moved[src][j])
                            sums[i][j] = part if sums[i][j] is None else sums[i][j] + part
                bg_ref[r + 1, own, :] = jnp.where(keep, back, 0.0)
            packed = jnp.zeros((8, 128), F32)
            for i in range(3):
                for j in range(3):
                    packed = jnp.where(lanes == 3 * i + j, jnp.sum(sums[i][j], axis=1, keepdims=True), packed)
            gk_ref[own, :] = packed
        return carry

    lax.fori_loop(0, ch // 8, group, 0, unroll=True)
    acc = None
    for r in range(rows + 2):
        normed = halo_ref[0] if r == 0 else halo_ref[1] if r == rows + 1 else normed_of(band_ref[r - 1])[0]
        term = outer_pixels(normed, bg_ref[r])
        acc = term if acc is None else acc + term
    project(odd_ref, bg_ref, exp_ref, dn_ref, first_ref, second_ref)
    at = gradb_ref.shape[0]
    all_ref[0:at, :] = gradb_ref[...]
    all_ref[at : at + ch, :] = fold(acc)
    all_ref[at + ch : at + ch + 16, :] = gk_ref[...].T[0:16, :]
    at = at + ch + 16
    if at < all_ref.shape[0]:
        all_ref[at : all_ref.shape[0], :] = jnp.zeros((all_ref.shape[0] - at, wide), F32)
    core = core_ref[0]
    place = 0
    for ref in (all_ref, own_ref, other_ref):
        lines = ref.shape[0] // 2
        at = slice(place, place + lines)
        mine_ref[at, :] = ref[pl.ds(pl.multiple_of(lines * core, 8), lines), :]
        theirs_ref[at, :] = ref[pl.ds(pl.multiple_of(lines * (1 - core), 8), lines), :]
        place += lines


def project(odd_ref, bg_ref, exp_ref, dn_ref, first_ref, second_ref):
    rows = dn_ref.shape[0]
    weight = left_lanes(exp_ref[...])
    above, *own, below = [dot_nn(weight, right_rows(bg_ref[r])) for r in range(rows + 2)]
    odd = odd_ref[0] == 1
    first_ref[...] = jnp.where(odd, above, below)
    second_ref[...] = jnp.where(odd, below, above)
    for r in range(rows):
        dn_ref[r] = own[r]


def place_rows(o_ref, row, value):
    o_ref[:, row, :] = value[:, 0 : o_ref.shape[2]]


def collect(view_ref, scratch_ref, kept, sent):
    half = scratch_ref.shape[0] // 2
    for k in range(half):
        scratch_ref[base_of(view_ref, half, True) + k] = kept[k]
        scratch_ref[base_of(view_ref, half, False) + k] = sent[k]


def front_back_kernel(half, view_ref, odd_ref, dn_ref, first_ref, second_ref, band_ref, keep_ref, *refs):
    sends, (o_ref, scratch_ref) = refs[:half], refs[half:]
    rows = dn_ref.shape[0]
    collect(view_ref, scratch_ref, keep_ref, [ref[0] for ref in sends])
    for h in range(rows):
        dn = dn_ref[h]
        if h == 0:
            dn = dn + jnp.where(odd_ref[0] == 1, first_ref[...], second_ref[...])
        if h == rows - 1:
            dn = dn + jnp.where(odd_ref[0] == 1, second_ref[...], first_ref[...])
        normed, spread = normed_of(band_ref[h])
        place_rows(o_ref, h, scratch_ref[h] + norm_back(dn, normed, spread))


def assemble_kernel(half, view_ref, sent_ref, *refs):
    keeps, (o_ref, scratch_ref) = refs[:half], refs[half:]
    collect(view_ref, scratch_ref, [ref[...] for ref in keeps], sent_ref)
    for h in range(2 * half):
        place_rows(o_ref, h, scratch_ref[h])


def finish_kernel(
    factor,
    slots,
    core_ref,
    mine_ref,
    theirs_ref,
    up_ref,
    down_ref,
    squeeze_ref,
    pool_ref,
    bias_ref,
    branch_ref,
    scale_ref,
    exp_ref,
    k_ref,
    q_ref,
    v_ref,
    s_ref,
    all_ref,
    own_ref,
):
    ch = q_ref.shape[0]
    core = core_ref[0]
    place = 0
    for ref in (all_ref, own_ref):
        lines = ref.shape[0] // 2
        at = slice(place, place + lines)
        ref[pl.ds(pl.multiple_of(lines * core, 8), lines), :] = mine_ref[at, :] * factor
        ref[pl.ds(pl.multiple_of(lines * (1 - core), 8), lines), :] = theirs_ref[at, :] * factor
        place += lines
    up_ref[...] = all_ref[0:ch, :]
    down_ref[...] = all_ref[ch : 2 * ch, 0:ch]
    squeeze_ref[...] = all_ref[ch : 2 * ch, ch : 2 * ch]
    at = 2 * ch
    slots = all_ref[at : at + slots, :]
    pool_ref[...] = lax.dot_general(
        slots[:, 0:ch],
        slots[:, ch : 2 * ch] * (1.0 / factor),
        (((0,), (0,)), ((), ())),
        precision=lax.Precision.HIGHEST,
        preferred_element_type=F32,
    )
    bias_ref[...] = jnp.sum(slots[:, 0:ch], axis=0, keepdims=True)
    at = at + slots.shape[0]
    branch_ref[...] = all_ref[at : at + 1, 0:ch]
    scale_ref[...] = all_ref[at : at + 1, ch : 2 * ch]
    at = at + 8
    exp_ref[...] = all_ref[at : at + ch, :]
    at = at + ch
    for i in range(3):
        k_ref[i] = all_ref[at + 3 * i : at + 3 * i + 3, :]
    q_ref[...] = own_ref[0:ch, 0:ch]
    v_ref[...] = own_ref[0:ch, ch : 2 * ch]
    s_ref[...] = own_ref[ch : ch + 1, 0:ch]


def add_kernel(mine_ref, other_ref, o_ref):
    o_ref[...] = mine_ref[...] + other_ref[...]


def add_split_kernel(mine_ref, other_ref, keep_ref, send_ref):
    total, both = mine_ref.shape[0], keep_ref.shape[0]
    owned = total - both
    keep_ref[...] = mine_ref[0:both, :] + other_ref[0:both, :]
    send_ref[0 : both - owned, :] = keep_ref[0 : both - owned, :]
    send_ref[both - owned : both, :] = mine_ref[both:total, :] + other_ref[both:total, :]


def call(kernel, outs, *args, scalars=0, far=0, scratch=(), aliases=None, limit=12 * MIB):
    smem = pl.BlockSpec(memory_space=pltpu.SMEM)
    vmem = pl.BlockSpec(memory_space=pltpu.VMEM)
    hbm = pl.BlockSpec(memory_space=pltpu.HBM)
    shapes = tuple(jax.ShapeDtypeStruct(s, F32) for s in outs)
    return pl.pallas_call(
        kernel,
        out_shape=shapes,
        in_specs=[smem] * scalars + [hbm] * far + [vmem] * (len(args) - scalars - far),
        out_specs=(vmem,) * len(shapes),
        scratch_shapes=list(scratch),
        compiler_params=pltpu.CompilerParams(vmem_limit_bytes=limit),
        input_output_aliases=aliases or {},
    )(*args)


def swap(x, axis, mask):
    return lax.ppermute(x, axis, [(i, i ^ mask) for i in range(lax.axis_size(axis))])


def add(x, y):
    return call(add_kernel, [x.shape], x, y)[0]


def sum_over(x, axis, first=1):
    size, mask = lax.axis_size(axis), first
    if size & (size - 1):
        raise ValueError("axis size")
    while mask < size:
        x = add(x, swap(x, axis, mask))
        mask *= 2
    return x


def parts_over(x, axis):
    if lax.axis_size(axis) > 4:
        return (sum_over(x, axis),)
    return (x,) + tuple(swap(x, axis, mask) for mask in range(1, lax.axis_size(axis)))


def per_device(
    frames_in,
    cotangent,
    expand_in,
    conv_kernel,
    pool_proj,
    pool_bias,
    squeeze_out,
    branch_scale,
    ffn_expand,
    ffn_shrink,
    ffn_scale,
    query_proj,
    value_proj,
    cross_scale,
):
    _, frames, ch, rows, width = frames_in.shape
    assert frames == 1 and rows % 2 == 0
    half = rows // 2
    wide = 2 * ch
    padded = -(-width // 128) * 128
    bands = lax.axis_size("row")
    area = rows * bands * width
    factor = (2 * frames * lax.axis_size("dp") * area) ** (-0.5)
    view = lax.axis_index("view").astype(jnp.int32).reshape(1)
    core = (lax.axis_index("dp").astype(jnp.int32) & 1).reshape(1)
    odd = (lax.axis_index("row").astype(jnp.int32) & 1).reshape(1)
    slot = (2 * lax.axis_index("dp") + lax.axis_index("view")).astype(jnp.int32).reshape(1)
    slots = -(-2 * lax.axis_size("dp") // 8) * 8
    part, full = (half, ch, padded), (rows, ch, padded)
    row = (ch, padded)
    exp_t, up_t = expand_in.T, ffn_expand.T
    k_rows = jnp.transpose(conv_kernel, (1, 2, 0))
    bias, branch, scale = (x.reshape(1, ch) for x in (pool_bias, branch_scale, ffn_scale))
    vm = lambda *shape: pltpu.VMEM(shape, F32)

    lines = half * ch + wide * ch // padded + 8
    query, value = query_proj[0], value_proj[0]
    band, border0, border1 = call(start_kernel, [full, row, row], view, core, odd, slot, frames_in[0, 0], scalars=4)
    pairs = [
        [pair for i in range(begin, bands - 1, 2) for pair in ((i, i + 1), (i + 1, i))] for begin in range(2)
    ]

    def meet(x, turn):
        return lax.ppermute(x, "row", pairs[turn])

    border0 = meet(border0, 0)
    border1 = meet(border1, 1)
    square, line = (ch, ch), (1, ch)
    fars = (query, value, cross_scale, pool_proj, bias, squeeze_out, branch, up_t, ffn_shrink, scale, exp_t, k_rows)
    cot_keep, pack, *nears = call(
        functools.partial(pack_kernel, len(fars)),
        [part, (lines, padded)] + [x.shape for x in fars],
        view,
        *(pltpu.with_memory_space_constraint(x, pltpu.HBM) for x in fars),
        cotangent[0, 0],
        scalars=1,
        far=len(fars),
        scratch=[vm(rows, ch, padded), pltpu.SemaphoreType.DMA((len(fars),))],
    )
    query, value, cross, pool_proj, bias, squeeze_out, branch, up_t, ffn_shrink, scale, exp_t, k_rows = nears
    other = swap(pack, "view", 1)
    doubled, conv, gating, pool, taps = call(
        functools.partial(conv_own_kernel, width),
        [(rows, wide, padded)] * 2 + [full, row, (wide, wide)],
        band,
        exp_t,
        k_rows,
    )
    conv, gating, edge, halo, pool = call(
        functools.partial(conv_edge_kernel, width),
        [(rows, wide, padded), full, (2, wide, padded), (2, ch, padded), (8, wide)],
        odd,
        conv,
        gating,
        pool,
        taps,
        border0,
        border1,
        exp_t,
        scalars=1,
        scratch=[vm(ch, 128)],
        aliases={1: 0, 2: 1},
    )
    pools = parts_over(pool, "row")
    parts = len(pools)
    inner = (squeeze_out, branch, up_t, ffn_shrink, scale)

    every = range(half)

    def tail(kept, picks, gate):
        count = len(picks)
        first = len(gate) > 1
        return call(
            functools.partial(tail_kernel, area, kept, picks, parts if first else 0),
            [(count, ch, padded), (count, wide, padded)] + [row] * count + [(8, ch)] * first,
            view,
            band,
            gating,
            *gate,
            *inner,
            scalars=1,
        )

    sent, hid_other = [], []
    gate = pools + (pool_proj, bias)
    for k in every:
        one, expanded, hidden, *attention = tail(False, (k,), gate)
        gate = tuple(attention) or gate
        sent.append((one, expanded))
        hid_other.append(swap(hidden, "view", 1))
    one_keep, expanded_keep, *hid_keep = tail(True, tuple(every), gate)
    out_keep, dh_keep, dh_back, terms = [], [], [], []
    out_send = ()
    for k in every:
        out, out_send, dh, dh_send, term = call(
            functools.partial(attend_kernel, width, k),
            [row, (k + 1, ch, padded), row, row, (6, ch, padded)],
            hid_keep[k],
            hid_other[k],
            cot_keep,
            query,
            value,
            cross,
            other,
            *((out_send,) if k else ()),
            scratch=[vm(padded, padded), pltpu.VMEM((padded, padded), BF16), pltpu.VMEM((padded, padded), BF16)],
        )
        out_keep.append(out)
        dh_keep.append(dh)
        terms.append(term)
        dh_back.append(swap(dh_send, "view", 1))
    out_back = swap(out_send, "view", 1)
    grad_own, grad_other = call(
        functools.partial(attend_grads_kernel, half), [(ch + 16, wide)] * 2, *terms, *hid_keep, *hid_other
    )

    def tail_back(kept, picks, final, one, expanded, dh, acc):
        count = len(picks)
        return call(
            functools.partial(tail_back_kernel, area, kept, picks, acc is None, final),
            [(count, ch, padded)] * 2 + [(wide, 8 * ch)] + [(8, wide)] * final,
            view,
            gating,
            one,
            expanded,
            *dh,
            *gate,
            *inner,
            *(() if acc is None else (acc,)),
            *((pool_proj,) if final else ()),
            scalars=1,
        )

    dgate_keep, done_keep, acc = tail_back(True, tuple(every), False, one_keep, expanded_keep, dh_keep, None)
    dgate_send, done_send = [], []
    for k in every:
        final = k == half - 1
        dgate, done, acc, *pool_grad = tail_back(False, (k,), final, *sent[k], [dh_back[k]], acc)
        dgate_send.append(dgate)
        done_send.append(done)
    (pool_grad,) = pool_grad
    (grad_b,) = call(
        functools.partial(tail_grads_kernel, area),
        [(2 * ch + slots + 8, wide)],
        slot,
        acc,
        *gate,
        squeeze_out,
        branch,
        ffn_shrink,
        scale,
        pool,
        scalars=1,
    )
    pool_grads = parts_over(pool_grad, "row")
    (output,) = call(
        functools.partial(assemble_kernel, half),
        [(ch, rows, width)],
        view,
        out_back,
        *out_keep,
        scalars=1,
        scratch=[vm(rows, ch, padded)],
    )
    shared_lines = -(-(2 * ch + slots + 8 + ch + 16) // 16) * 16
    owned_lines = ch + 16
    piece = shared_lines // 2 + owned_lines
    dn, border0, border1, mine, theirs = call(
        functools.partial(conv_back_kernel, width, len(pool_grads), half),
        [full, row, row, (piece, wide), (piece, wide)],
        view,
        core,
        odd,
        *pool_grads,
        *dgate_send,
        grad_own,
        grad_other,
        dgate_keep,
        conv,
        doubled,
        edge,
        band,
        halo,
        exp_t,
        taps,
        grad_b,
        scalars=3,
        scratch=[vm(shared_lines, wide), vm(rows + 2, wide, padded), vm(rows, ch, padded), vm(wide, wide), vm(ch, wide)],
    )
    border0 = meet(border0, 0)
    border1 = meet(border1, 1)
    both = (shared_lines + owned_lines) // 2
    mine, send = call(add_split_kernel, [(both, wide)] * 2, mine, swap(theirs, "dp", 1))
    mine = add(mine, swap(send, "view", 1))
    mine = sum_over(mine, "dp", 2)
    mine = sum_over(mine, "row")
    theirs = swap(mine, "dp", 1)
    (frames_grad,) = call(
        functools.partial(front_back_kernel, half),
        [(ch, rows, width)],
        view,
        odd,
        dn,
        border0,
        border1,
        band,
        done_keep,
        *done_send,
        scalars=2,
        scratch=[vm(rows, ch, padded)],
    )
    g_up, g_down, g_squeeze, g_pool, g_bias, g_branch, g_scale, g_exp, g_k, g_q, g_v, g_s = call(
        functools.partial(finish_kernel, factor, slots),
        [(ch, wide), square, square, square, line, line, line, (ch, wide), (3, 3, wide), square, square, line],
        core,
        mine,
        theirs,
        scalars=1,
        scratch=[vm(shared_lines, wide), vm(owned_lines, wide)],
    )
    return (
        output[None, None],
        frames_grad[None, None],
        g_exp.T,
        jnp.transpose(g_k, (2, 0, 1)),
        g_pool,
        g_bias.reshape(ch),
        g_squeeze,
        g_branch.reshape(ch),
        g_up.T,
        g_down,
        g_scale.reshape(ch),
        g_q[None],
        g_v[None],
        g_s,
    )


def solution(mesh):
    image = P("view", "dp", None, "row", None)
    owned = (P("view", None, None), P("view", None, None), P("view", None))

    return jax.shard_map(
        per_device,
        mesh=mesh,
        in_specs=(image, image) + (P(),) * 9 + owned,
        out_specs=(image, image) + (P(),) * 9 + owned,
        check_vma=False,
    )
```
